256 devices in a mesh: gy: 8 (over y, core), gx: 32 (over x, z).
Axes of the slice: x: 4, y: 4, z: 8, core: 2. Of those that a mesh axis runs over, the one named last changes fastest.
Arguments:
- phase: float32 [2, 256, 4096], P(None, 'gy', 'gx'), may hold values from -1.5 to 1.5
- velocity: float32 [2, 256, 4096], P(None, 'gy', 'gx'), may hold values from -2 to 2
- offsets: int32 [2, 8], replicated, may hold values from 0 to 4092, as said below
Outputs:
- phase_out: float32 [2, 256, 4096], P(None, 'gy', 'gx')
The draws below stay inside these ranges and needn't reach their ends.
Inputs may be any that keep to these rules, and one draw needn't show every extreme that they name: `offsets`: every offset is a multiple of 2 ** 2.
All inputs are finite; a program needn't handle non-finite values.
Results may differ from the reference program's by a relative error of at most 0.00014.
Values sent between devices are 32-bit elements; how exact they have to be, the bound alone decides.
A program may use at most 64 MiB of HBM per device.

```python
import jax
import jax.numpy as jnp

CY = 32
NZ = 2
STEPS = 2
ITERS = 2
LEVELS = 3
COARSE = 4
NX = 4096
NY = 256
N_GY = 8


def draw_offsets(key, part):
    spacing = 2 ** (LEVELS - 1)
    return jax.random.randint(key, (STEPS, N_GY), 0, NX // spacing, dtype=jnp.int32) * spacing


def levels(own_key, shape, shards, least, top_value):
    loudness, own = 1.0, jax.random.fold_in(own_key, 6)
    for position, parts in shards:
        heights = jnp.exp(jax.random.uniform(jax.random.fold_in(own, position), (parts,), jnp.float32, least / len(shards), top_value / len(shards)))
        loudness = loudness * jnp.repeat(heights, shape[position] // parts).reshape([-1 if axis == position else 1 for axis in range(len(shape))])
    return loudness


def setup_inputs(seed: int = 0) -> dict:
    splits = jax.random.split(jax.random.key(seed), 4)
    return {
        "phase": jnp.clip(jax.random.uniform(splits[0], (NZ, NY, NX), jnp.float32, -1.5, 1.5) * levels(splits[0], (NZ, NY, NX), ((1, 8), (2, 32)), -0.4, 0.0), -1.5, 1.5),
        "velocity": jnp.clip(jax.random.uniform(splits[1], (NZ, NY, NX), jnp.float32, -2.0, 2.0) * levels(splits[1], (NZ, NY, NX), ((1, 8), (2, 32)), -0.4, 0.0), -2.0, 2.0),
        "offsets": draw_offsets(jax.random.fold_in(splits[3], 71), 0),
    }


RELAXATION = 0.8
DIFFUSION = 4.0
VERTICAL = 1.0
REACTION = 0.5
ADVECTION = 0.5


def neighbours(field, offsets_now, block_rows):
    planes, height, breadth = field.shape
    blocks = field.reshape(planes, N_GY, block_rows, breadth)
    columns = jnp.arange(breadth, dtype=jnp.int32)
    first_rows = blocks[:, :, 0, :]
    last_rows = blocks[:, :, -1, :]
    next_first = jnp.roll(first_rows, -1, axis=1)
    next_offsets = jnp.roll(offsets_now, -1)
    upper_index = (columns[None, :] + next_offsets[:, None]) % breadth
    above_rows = jnp.take_along_axis(next_first, jnp.broadcast_to(upper_index[None], next_first.shape), axis=2)
    previous_last = jnp.roll(last_rows, 1, axis=1)
    lower_index = (columns[None, :] - offsets_now[:, None]) % breadth
    below_rows = jnp.take_along_axis(previous_last, jnp.broadcast_to(lower_index[None], previous_last.shape), axis=2)
    upward = jnp.concatenate([blocks[:, :, 1:, :], above_rows[:, :, None, :]], axis=2).reshape(planes, height, breadth)
    downward = jnp.concatenate([below_rows[:, :, None, :], blocks[:, :, :-1, :]], axis=2).reshape(planes, height, breadth)
    return upward + downward + jnp.roll(field, 1, 2) + jnp.roll(field, -1, 2)


def operate(field, offsets_now, block_rows, coupling):
    diagonal = 1.0 + 4.0 * coupling + 2.0 * VERTICAL
    vertical_sum = jnp.roll(field, 1, 0) + jnp.roll(field, -1, 0)
    return diagonal * field - coupling * neighbours(field, offsets_now, block_rows) - VERTICAL * vertical_sum


def vcycle(residual, offsets_raw, layer_index):
    factor = 2 ** layer_index
    coupling = DIFFUSION / 4.0 ** layer_index
    diagonal = 1.0 + 4.0 * coupling + 2.0 * VERTICAL
    offsets_now = (offsets_raw // factor).astype(jnp.int32)
    block_rows = CY // factor
    estimate = RELAXATION * residual / diagonal
    if layer_index == LEVELS - 1:
        for sweep_index in range(COARSE - 1):
            estimate = estimate + RELAXATION * (residual - operate(estimate, offsets_now, block_rows, coupling)) / diagonal
        return estimate
    defect = residual - operate(estimate, offsets_now, block_rows, coupling)
    planes, height, breadth = defect.shape
    coarser = defect.reshape(planes, height // 2, 2, breadth // 2, 2).mean(axis=(2, 4))
    correction = vcycle(coarser, offsets_raw, layer_index + 1)
    estimate = estimate + jnp.repeat(jnp.repeat(correction, 2, axis=1), 2, axis=2)
    estimate = estimate + RELAXATION * (residual - operate(estimate, offsets_now, block_rows, coupling)) / diagonal
    return estimate


def reference(phase, velocity, offsets):
    phase_now = phase
    for time_step in range(STEPS):
        offsets_raw = offsets[time_step]
        source = phase_now + REACTION * (phase_now - phase_now * phase_now * phase_now) - ADVECTION * velocity * (jnp.roll(phase_now, -1, 2) - jnp.roll(phase_now, 1, 2))
        residual = source - operate(phase_now, offsets_raw, CY, DIFFUSION)
        precond = vcycle(residual, offsets_raw, 0)
        projected = jnp.sum(residual * precond)
        direction = precond
        for iteration in range(ITERS):
            image = operate(direction, offsets_raw, CY, DIFFUSION)
            step_size = projected / jnp.sum(direction * image)
            phase_now = phase_now + step_size * direction
            residual = residual - step_size * image
            if iteration + 1 < ITERS:
                precond = vcycle(residual, offsets_raw, 0)
                following = jnp.sum(residual * precond)
                direction = precond + (following / projected) * direction
                projected = following
    return phase_now
```

```python
import jax
import jax.numpy as jnp
from jax import lax
from jax.experimental import pallas as pl
from jax.experimental.pallas import tpu as pltpu
from jax.sharding import PartitionSpec as P

MESH = pl.DeviceIdType.MESH
NGY, NGX = 8, 32
RELAX, DIFFUSION, REACTION, ADVECTION = 0.8, 4.0, 0.5, 0.5
COUPLING = [DIFFUSION / 4.0**level for level in range(3)]
DIAGONAL = [1.0 + 4.0 * c + 2.0 for c in COUPLING]
SCALE = [RELAX / d for d in DIAGONAL]
COARSE = 4


def lanes(shape=(8, 128)):
    return lax.broadcasted_iota(jnp.int32, shape, len(shape) - 1)


def lane_roll(v, shift):
    return pltpu.roll(v, shift, 1)


def right_of(v):
    last = lane_roll(v[0], 127)[None]
    return last if v.shape[0] == 1 else jnp.concatenate([v[1:], last], axis=0)


def left_of(v):
    first = lane_roll(v[v.shape[0] - 1], 1)[None]
    return first if v.shape[0] == 1 else jnp.concatenate([first, v[:-1]], axis=0)


def sub_roll(v, shift):
    return jnp.stack([pltpu.roll(v[k], shift, 0) for k in range(v.shape[0])])


def vertical(rows):
    count = len(rows)
    after = rows[1:] + [sub_roll(rows[0], 7)]
    before = [sub_roll(rows[count - 1], 1)] + rows[:-1]
    return [a + b for a, b in zip(after, before)]


def beside(rows):
    return [s + (right_of(v) + left_of(v)) for s, v in zip(vertical(rows), rows)]


def coarser(rows):
    out = []
    for r in range(0, len(rows), 2):
        s = rows[r] + rows[r + 1]
        out.append(0.25 * jnp.stack([s[k] + s[k + 1] for k in range(0, s.shape[0], 2)]))
    return out


def finer(rows):
    out = []
    for v in rows:
        wide = jnp.stack([v[k // 2] for k in range(2 * v.shape[0])])
        out += [wide, wide]
    return out


def of_planes(total, difference):
    return jnp.where(lanes() < 64, jnp.float32(total), jnp.float32(difference))


def mixed(v):
    other = jnp.stack([lane_roll(v[k], 64) for k in range(v.shape[0])])
    return jnp.where((lanes() < 64)[None], v + other, other - v)


def operate(rows):
    d = of_planes(DIAGONAL[0] - 2.0, DIAGONAL[0] + 2.0)
    return [d * v - COUPLING[0] * b for v, b in zip(rows, beside(rows))]


def smoothing(level):
    d, s = DIAGONAL[level], SCALE[level]
    return s, of_planes(1.0 - s * (d - 2.0), 1.0 - s * (d + 2.0)), s * COUPLING[level]


def precondition(rows, level=0):
    scale, keep, spread = smoothing(level)
    if level == 2:
        base = [scale * v for v in rows]
        e = base
        for _ in range(COARSE - 1):
            e = [f + keep * v + spread * b for f, v, b in zip(base, e, beside(e))]
        return e
    defect = [keep * v + spread * b for v, b in zip(rows, beside(rows))]
    correction = finer(precondition(coarser(defect), level + 1))
    e = [scale * v + c for v, c in zip(rows, correction)]
    return [scale * f + keep * v + spread * b for f, v, b in zip(rows, e, beside(e))]


def residual_of(u, v):
    out = []
    for s, f, speed in zip(vertical(u), u, v):
        east, west = right_of(f), left_of(f)
        around = s + (east + west)
        source = f + REACTION * (f - f * f * f) - ADVECTION * speed * (east - west)
        other = jnp.stack([lane_roll(f[k], 64) for k in range(4)])
        applied = DIAGONAL[0] * f - COUPLING[0] * around - 2.0 * other
        out.append(mixed(source - applied))
    return out


def own_sum(first, second):
    total = None
    for a, b in zip(first, second):
        product = a * b
        part = (product[0] + product[1]) + (product[2] + product[3])
        total = part if total is None else total + part
    m = lanes() & 63
    total = jnp.where((m >= 16) & (m < 48), total, 0.0)
    return total[3:4] + total[4:5]


def packed_sums(pairs):
    sums = [own_sum(a, b) for a, b in pairs]
    tile = jnp.concatenate(sums + [jnp.zeros((8 - len(sums), 128), jnp.float32)], axis=0)
    for shift in (64, 32, 16):
        tile = tile + lane_roll(tile, shift)
    row = lax.broadcasted_iota(jnp.int32, (8, 128), 0)
    return jnp.sum(jnp.where((lanes() >> 4) == row, tile, 0.0), axis=0, keepdims=True)


def coefficients(packed):
    group = lanes((1, 128)) >> 4
    rw, wq, rz, qz, zy = (
        jnp.sum(jnp.where(group == d, packed, 0.0), axis=1, keepdims=True) for d in range(5)
    )
    a0 = rw / wq
    following = a0 * (a0 * qz - rz)
    b = 1.0 + following / rw
    a1 = following / (b * b * wq - 2.0 * b * a0 * qz + a0 * a0 * zy)
    return a0 + a1 * b, -a1 * a0


def permuted(x, matrix):
    n = x.shape[0]
    high = x.astype(jnp.bfloat16)
    rest = x - high.astype(jnp.float32)
    mid = rest.astype(jnp.bfloat16)
    low = (rest - mid.astype(jnp.float32)).astype(jnp.bfloat16)
    y = jnp.dot(jnp.concatenate([high, mid, low], axis=0), matrix, preferred_element_type=jnp.float32)
    return (y[:n] + y[n : 2 * n]) + y[2 * n :]


def kernel(
    offsets, phase, velocity, out,
    own, got, spread, west, east, sent, later, third, window, ahead, stage,
    own2, got2, west2, east2, window2,
    part, part_row, sums_row, sums_col, part2, part2_row, sums2_row, sums2_col,
    ssem, rsem, s2sem, r2sem,
):
    j, i = lax.axis_index("gy"), lax.axis_index("gx")
    field, pair = i // 16, lax.rem(i, 16)
    up, down = lax.rem(j + 1, NGY), lax.rem(j + NGY - 1, NGY)
    up2, down2 = lax.rem(j + 2, NGY), lax.rem(j + NGY - 2, NGY)
    far = (pair < 4) | (pair >= 12)
    far_row = jnp.where(pair < 4, down2, up2)
    far_slot = field * 64 + jnp.where(pair < 4, 56 + pair, pair - 8)
    near_west, near_east = lax.rem(i + NGX - 1, NGX), lax.rem(i + 1, NGX)

    def tile(ref, slot, count=1):
        return ref.at[pl.ds(pl.multiple_of(slot * 8, 8), 8 * count)]

    def copy(src, dst, ss, rs, row, column):
        return pltpu.make_async_remote_copy(
            src_ref=src, dst_ref=dst, send_sem=ss, recv_sem=rs, device_id=(row, column), device_id_type=MESH
        )

    def to_row(src, dst, ss, rs):
        def body(d, carry):
            q = lax.rem(i + d, NGX)
            copy(tile(src, q), tile(dst, i), ss, rs, j, q).start()
            return carry

        lax.fori_loop(1, NGX, body, 0)
        dst[pl.ds(pl.multiple_of(i * 8, 8), 8), :] = src[pl.ds(pl.multiple_of(i * 8, 8), 8), :]

    def to_sides(src, dst_west, dst_east, sems):
        copy(src, dst_west, ssem.at[sems], rsem.at[sems], j, near_east).start()
        copy(src, dst_east, ssem.at[sems + 1], rsem.at[sems + 1], j, near_west).start()

    def all_tiles(ref, count, ss, rs):
        return copy(ref.at[pl.ds(0, 8 * count)], ref.at[pl.ds(0, 8 * count)], ss, rs, j, near_east)

    def to_spread(src):
        here = src[...]
        following = jnp.concatenate([here[8:], here[:8]], axis=0)
        m = lanes((256, 128)) & 63
        spread[...] = jnp.where(m < 32, here, lane_roll(following, 32))

    def to_windows(dst, variant, shift):
        start = lax.rem(shift // 4 + (4096 - 16), 1024)
        block, g = start // 32, lax.rem(start, 32)
        near = spread[...].reshape(32, 8, 128)
        whole = jnp.full((8, 128), block, jnp.int32)
        for bit in range(5):
            step = 1 << bit
            ahead_of = jnp.concatenate([near[step:], near[:step]], axis=0)
            near = jnp.where(((whole & step) != 0)[None], ahead_of, near)
        next_ = jnp.concatenate([near[2:], near[:2]], axis=0)
        m = lanes((256, 128)) & 63
        near, next_ = near.reshape(256, 128), next_.reshape(256, 128)
        dst[pl.ds(variant * 256, 256), :] = jnp.where(
            m + g < 64, lane_roll(near, lax.rem(128 - g, 128)), lane_roll(next_, 64 - g)
        )

    def shifts(step):
        above, below = offsets[step, up], offsets[step, j]
        second = jnp.where(pair < 4, below + offsets[step, down], -(above + offsets[step, up2]))
        return -above, below, second

    def to_windows_of(dst, step):
        for variant, shift in enumerate(shifts(step)):
            to_windows(dst, variant, shift)

    def to_columns(src, dst, ss, rs):
        def body(n, carry):
            c = lax.rem(i + n, NGX)
            copy(tile(src, c), tile(dst, field * 64 + 8 + pair), ss, rs, up, c).start()
            copy(tile(src, 32 + c), tile(dst, field * 64 + 40 + pair), ss, rs, down, c).start()
            return carry

        lax.fori_loop(0, NGX, body, 0)

        @pl.when(far)
        def _():
            def far_body(n, carry):
                c = lax.rem(i + n, NGX)
                copy(tile(src, 64 + c), tile(dst, far_slot), ss, rs, far_row, c).start()
                return carry

            lax.fori_loop(0, NGX, far_body, 0)

    def columns_sent(src, ss, rs):
        all_tiles(src, 64, ss, rs).wait_send()

        @pl.when(far)
        def _():
            all_tiles(src, 32, ss, rs).wait_send()

    def own_windows(centre, side_west, side_east, targets):
        m = lanes((128, 128)) & 63
        for f in range(2):
            at = pl.ds(128 * f, 128)
            whole = jnp.where(
                m < 16,
                lane_roll(side_west[at, :], 112),
                jnp.where(m < 48, lane_roll(centre[at, :], 16), lane_roll(side_east[at, :], 48)),
            )
            for target in targets:
                target[512 * f + 192 : 512 * f + 320, :] = whole

    def rows_of(ref, f):
        return [
            jnp.stack([ref[pl.ds(512 * f + 4 * r + k, 8, stride=64), :] for k in range(4)])
            for r in range(16)
        ]

    def put_rows(ref, f, rows):
        for r in range(16):
            for k in range(4):
                ref[pl.ds(512 * f + 4 * r + k, 8, stride=64), :] = rows[r][k]

    def sums_to_row(value, mine, dst, sems):
        mine[...] = value
        dst[i] = value

        def body(d, carry):
            q = lax.rem(i + d, NGX)
            copy(mine, dst.at[i], s2sem.at[sems], r2sem.at[sems], j, q).start()
            return carry

        lax.fori_loop(1, NGX, body, 0)

    def sums_to_col(value, mine, dst, sems):
        mine[...] = value
        dst[j] = value

        def body(d, carry):
            q = lax.rem(j + d, NGY)
            copy(mine, dst.at[j], s2sem.at[sems], r2sem.at[sems], q, i).start()
            return carry

        lax.fori_loop(1, NGY, body, 0)

    def few(ref, count, sems):
        return copy(ref.at[pl.ds(0, count)], ref.at[pl.ds(0, count)], s2sem.at[sems], r2sem.at[sems], j, near_east)

    n = lanes((128, 512))
    c = lax.broadcasted_iota(jnp.int32, (128, 512), 0)
    matrix = jnp.where(c == 4 * (n & 127) + (n >> 7), 1.0, 0.0).astype(jnp.bfloat16)
    blocks = jnp.concatenate([phase[0], phase[1], velocity[0], velocity[1]], axis=0)
    split = permuted(blocks, matrix)
    for f in range(2):
        for k in range(4):
            cut = split[64 * f : 64 * f + 64, 128 * k : 128 * k + 128]
            own[pl.ds(128 * f + k, 32, stride=4), :] = cut[:32] + lane_roll(cut[32:], 64)

    to_row(own, got, ssem.at[0], rsem.at[0])
    to_sides(own, west, east, 1)
    for ref in (window, ahead, window2):
        for f in range(2):
            ref[512 * f : 512 * f + 32, :] = jnp.zeros((32, 128), jnp.float32)
            ref[512 * f + 480 : 512 * f + 512, :] = jnp.zeros((32, 128), jnp.float32)
    all_tiles(got, 31, ssem.at[0], rsem.at[0]).wait_recv()
    to_spread(got)
    to_windows_of(sent, 0)
    to_columns(sent, window, ssem.at[3], rsem.at[3])
    to_windows_of(later, 1)
    to_columns(later, ahead, ssem.at[4], rsem.at[4])
    all_tiles(west, 32, ssem.at[1], rsem.at[1]).wait_recv()
    all_tiles(east, 32, ssem.at[2], rsem.at[2]).wait_recv()
    own_windows(own, west, east, (window, ahead))
    all_tiles(window, 80, ssem.at[3], rsem.at[3]).wait_recv()

    def solve(u, v):
        r = residual_of(u, v)
        w = precondition(r)
        q = operate(w)
        z = precondition(q)
        y = operate(z)
        return w, z, packed_sums(((r, w), (w, q), (r, z), (q, z), (z, y)))

    w, z, packed = solve(rows_of(window, 0), rows_of(window, 1))
    put_rows(stage, 0, w)
    put_rows(stage, 1, z)
    for f in range(2):
        own2[128 * f : 128 * f + 128, :] = lane_roll(stage[512 * f + 192 : 512 * f + 320, :], 112)
    to_row(own2, got2, ssem.at[5], rsem.at[5])
    sums_to_row(packed, part, sums_row, 0)
    to_sides(own2, west2, east2, 6)
    all_tiles(got2, 31, ssem.at[5], rsem.at[5]).wait_recv()
    to_spread(got2)
    to_windows_of(third, 1)
    to_columns(third, window2, ssem.at[8], rsem.at[8])
    few(sums_row, 31, 0).wait_recv()
    sums_to_col(jnp.sum(sums_row[...], axis=0), part_row, sums_col, 1)
    all_tiles(west2, 32, ssem.at[6], rsem.at[6]).wait_recv()
    all_tiles(east2, 32, ssem.at[7], rsem.at[7]).wait_recv()
    own_windows(own2, west2, east2, (window2,))
    few(sums_col, 7, 1).wait_recv()
    c1, c2 = coefficients(jnp.sum(sums_col[...], axis=0))
    all_tiles(ahead, 80, ssem.at[4], rsem.at[4]).wait_recv()
    all_tiles(window2, 80, ssem.at[8], rsem.at[8]).wait_recv()

    def moved(u, w, z, c1, c2):
        return [a + 0.5 * mixed(c1 * b + c2 * d) for a, b, d in zip(u, w, z)]

    u = moved(rows_of(ahead, 0), rows_of(window2, 0), rows_of(window2, 1), c1, c2)
    w, z, packed = solve(u, rows_of(ahead, 1))
    sums_to_row(packed, part2, sums2_row, 2)
    few(sums2_row, 31, 2).wait_recv()
    sums_to_col(jnp.sum(sums2_row[...], axis=0), part2_row, sums2_col, 3)
    few(sums2_col, 7, 3).wait_recv()
    c1, c2 = coefficients(jnp.sum(sums2_col[...], axis=0))
    put_rows(stage, 0, moved(u, w, z, c1, c2))
    flat = jnp.concatenate([stage[pl.ds(192 + k, 32, stride=4), :] for k in range(4)], axis=1)
    rho = lax.broadcasted_iota(jnp.int32, (512, 256), 0)
    col = lanes((512, 256))
    c = col & 127
    back = ((rho >> 7) == (c & 3)) & ((rho & 127) == (col >> 7) * 64 + 16 + (c >> 2))
    flat = permuted(flat, jnp.where(back, 1.0, 0.0).astype(jnp.bfloat16))
    out[0] = flat[:, :128]
    out[1] = flat[:, 128:]

    all_tiles(own, 31, ssem.at[0], rsem.at[0]).wait_send()
    all_tiles(own, 32, ssem.at[1], rsem.at[1]).wait_send()
    all_tiles(own, 32, ssem.at[2], rsem.at[2]).wait_send()
    columns_sent(sent, ssem.at[3], rsem.at[3])
    columns_sent(later, ssem.at[4], rsem.at[4])
    all_tiles(own2, 31, ssem.at[5], rsem.at[5]).wait_send()
    all_tiles(own2, 32, ssem.at[6], rsem.at[6]).wait_send()
    all_tiles(own2, 32, ssem.at[7], rsem.at[7]).wait_send()
    columns_sent(third, ssem.at[8], rsem.at[8])
    few(sums_row, 31, 0).wait_send()
    few(sums_col, 7, 1).wait_send()
    few(sums2_row, 31, 2).wait_send()
    few(sums2_col, 7, 3).wait_send()


def local(phase, velocity, offsets):
    f32 = jnp.float32
    tiles = lambda count: pltpu.VMEM((8 * count, 128), f32)
    line, lines = pltpu.VMEM((1, 128), f32), lambda n: pltpu.VMEM((n, 1, 128), f32)
    vmem = pl.BlockSpec(memory_space=pltpu.VMEM)
    return pl.pallas_call(
        kernel,
        out_shape=jax.ShapeDtypeStruct(phase.shape, f32),
        in_specs=[pl.BlockSpec(memory_space=pltpu.SMEM), vmem, vmem],
        out_specs=vmem,
        scratch_shapes=[
            tiles(32), tiles(32), tiles(32), tiles(32), tiles(32), tiles(96), tiles(96), tiles(96), tiles(128), tiles(128), tiles(128),
            tiles(32), tiles(32), tiles(32), tiles(32), tiles(128),
            line, line, lines(32), lines(8), line, line, lines(32), lines(8),
            pltpu.SemaphoreType.DMA((9,)), pltpu.SemaphoreType.DMA((9,)),
            pltpu.SemaphoreType.DMA((4,)), pltpu.SemaphoreType.DMA((4,)),
        ],
        compiler_params=pltpu.CompilerParams(has_side_effects=True),
    )(offsets, phase, velocity)


def solution(mesh):
    return jax.shard_map(
        local,
        mesh=mesh,
        in_specs=(P(None, "gy", "gx"), P(None, "gy", "gx"), P()),
        out_specs=P(None, "gy", "gx"),
        check_vma=False,
    )
```

```python
import jax
import jax.numpy as jnp
from jax import lax
from jax.experimental import pallas as pl
from jax.experimental.pallas import tpu as pltpu
from jax.sharding import PartitionSpec as P

MESH = pl.DeviceIdType.MESH
NGY, NGX = 8, 32
RELAX, DIFFUSION, REACTION, ADVECTION = 0.8, 4.0, 0.5, 0.5
COUPLING = [DIFFUSION / 4.0**level for level in range(3)]
DIAGONAL = [1.0 + 4.0 * c + 2.0 for c in COUPLING]
SCALE = [RELAX / d for d in DIAGONAL]
COARSE = 4


def lanes(shape=(8, 128)):
    return lax.broadcasted_iota(jnp.int32, shape, len(shape) - 1)


def lane_roll(v, shift):
    return pltpu.roll(v, shift, 1)


def right_of(v):
    last = lane_roll(v[0], 127)[None]
    return last if v.shape[0] == 1 else jnp.concatenate([v[1:], last], axis=0)


def left_of(v):
    first = lane_roll(v[v.shape[0] - 1], 1)[None]
    return first if v.shape[0] == 1 else jnp.concatenate([first, v[:-1]], axis=0)


def sub_roll(v, shift):
    return jnp.stack([pltpu.roll(v[k], shift, 0) for k in range(v.shape[0])])


def vertical(rows):
    count = len(rows)
    after = rows[1:] + [sub_roll(rows[0], 7)]
    before = [sub_roll(rows[count - 1], 1)] + rows[:-1]
    return [a + b for a, b in zip(after, before)]


def beside(rows):
    return [s + (right_of(v) + left_of(v)) for s, v in zip(vertical(rows), rows)]


def coarser(rows):
    out = []
    for r in range(0, len(rows), 2):
        s = rows[r] + rows[r + 1]
        out.append(0.25 * jnp.stack([s[k] + s[k + 1] for k in range(0, s.shape[0], 2)]))
    return out


def finer(rows):
    out = []
    for v in rows:
        wide = jnp.stack([v[k // 2] for k in range(2 * v.shape[0])])
        out += [wide, wide]
    return out


def of_planes(total, difference):
    return jnp.where(lanes() < 64, jnp.float32(total), jnp.float32(difference))


def mixed(v):
    other = jnp.stack([lane_roll(v[k], 64) for k in range(v.shape[0])])
    return jnp.where((lanes() < 64)[None], v + other, other - v)


def operate(rows):
    d = of_planes(DIAGONAL[0] - 2.0, DIAGONAL[0] + 2.0)
    return [d * v - COUPLING[0] * b for v, b in zip(rows, beside(rows))]


def smoothing(level):
    d, s = DIAGONAL[level], SCALE[level]
    return s, of_planes(1.0 - s * (d - 2.0), 1.0 - s * (d + 2.0)), s * COUPLING[level]


def precondition(rows, level=0):
    scale, keep, spread = smoothing(level)
    if level == 2:
        base = [scale * v for v in rows]
        e = base
        for _ in range(COARSE - 1):
            e = [f + keep * v + spread * b for f, v, b in zip(base, e, beside(e))]
        return e
    defect = [keep * v + spread * b for v, b in zip(rows, beside(rows))]
    correction = finer(precondition(coarser(defect), level + 1))
    e = [scale * v + c for v, c in zip(rows, correction)]
    return [scale * f + keep * v + spread * b for f, v, b in zip(rows, e, beside(e))]


def residual_of(u, v):
    out = []
    for s, f, speed in zip(vertical(u), u, v):
        east, west = right_of(f), left_of(f)
        around = s + (east + west)
        source = f + REACTION * (f - f * f * f) - ADVECTION * speed * (east - west)
        other = jnp.stack([lane_roll(f[k], 64) for k in range(4)])
        applied = DIAGONAL[0] * f - COUPLING[0] * around - 2.0 * other
        out.append(mixed(source - applied))
    return out


def own_sum(first, second):
    total = None
    for a, b in zip(first, second):
        product = a * b
        part = (product[0] + product[1]) + (product[2] + product[3])
        total = part if total is None else total + part
    m = lanes() & 63
    total = jnp.where((m >= 16) & (m < 48), total, 0.0)
    return total[3:4] + total[4:5]


def packed_sums(pairs):
    sums = [own_sum(a, b) for a, b in pairs]
    tile = jnp.concatenate(sums + [jnp.zeros((8 - len(sums), 128), jnp.float32)], axis=0)
    for shift in (64, 32, 16):
        tile = tile + lane_roll(tile, shift)
    row = lax.broadcasted_iota(jnp.int32, (8, 128), 0)
    return jnp.sum(jnp.where((lanes() >> 4) == row, tile, 0.0), axis=0, keepdims=True)


def coefficients(packed):
    group = lanes((1, 128)) >> 4
    rw, wq, rz, qz, zy = (
        jnp.sum(jnp.where(group == d, packed, 0.0), axis=1, keepdims=True) for d in range(5)
    )
    a0 = rw / wq
    following = a0 * (a0 * qz - rz)
    b = 1.0 + following / rw
    a1 = following / (b * b * wq - 2.0 * b * a0 * qz + a0 * a0 * zy)
    return a0 + a1 * b, -a1 * a0


def permuted(x, matrix):
    n = x.shape[0]
    high = x.astype(jnp.bfloat16)
    rest = x - high.astype(jnp.float32)
    mid = rest.astype(jnp.bfloat16)
    low = (rest - mid.astype(jnp.float32)).astype(jnp.bfloat16)
    y = jnp.dot(jnp.concatenate([high, mid, low], axis=0), matrix, preferred_element_type=jnp.float32)
    return (y[:n] + y[n : 2 * n]) + y[2 * n :]


def kernel(
    offsets, phase, velocity, out,
    own, got, spread, west, east, sent, later, third, window, ahead, stage,
    own2, got2, west2, east2, window2,
    part, part_row, sums_row, sums_col, part2, part2_row, sums2_row, sums2_col,
    ssem, rsem, s2sem, r2sem, ready,
):
    j, i = lax.axis_index("gy"), lax.axis_index("gx")
    field, pair = i // 16, lax.rem(i, 16)
    up, down = lax.rem(j + 1, NGY), lax.rem(j + NGY - 1, NGY)
    up2, down2 = lax.rem(j + 2, NGY), lax.rem(j + NGY - 2, NGY)
    far = (pair < 4) | (pair >= 12)
    far_row = jnp.where(pair < 4, down2, up2)
    far_slot = field * 64 + jnp.where(pair < 4, 56 + pair, pair - 8)
    near_west, near_east = lax.rem(i + NGX - 1, NGX), lax.rem(i + 1, NGX)

    def tile(ref, slot, count=1):
        return ref.at[pl.ds(pl.multiple_of(slot * 8, 8), 8 * count)]

    def copy(src, dst, ss, rs, row, column):
        return pltpu.make_async_remote_copy(
            src_ref=src, dst_ref=dst, send_sem=ss, recv_sem=rs, device_id=(row, column), device_id_type=MESH
        )

    def to_row(src, dst, ss, rs):
        def body(d, carry):
            q = lax.rem(i + d, NGX)
            copy(tile(src, q), tile(dst, i), ss, rs, j, q).start()
            return carry

        lax.fori_loop(1, NGX, body, 0)
        dst[pl.ds(pl.multiple_of(i * 8, 8), 8), :] = src[pl.ds(pl.multiple_of(i * 8, 8), 8), :]

    def to_sides(src, dst_west, dst_east, sems):
        copy(src, dst_west, ssem.at[sems], rsem.at[sems], j, near_east).start()
        copy(src, dst_east, ssem.at[sems + 1], rsem.at[sems + 1], j, near_west).start()

    def all_tiles(ref, count, ss, rs):
        return copy(ref.at[pl.ds(0, 8 * count)], ref.at[pl.ds(0, 8 * count)], ss, rs, j, near_east)

    def to_spread(src):
        here = src[...]
        following = jnp.concatenate([here[8:], here[:8]], axis=0)
        m = lanes((256, 128)) & 63
        spread[...] = jnp.where(m < 32, here, lane_roll(following, 32))

    def to_windows(dst, variant, shift):
        start = lax.rem(shift // 4 + (4096 - 16), 1024)
        block, g = start // 32, lax.rem(start, 32)
        near = spread[...].reshape(32, 8, 128)
        whole = jnp.full((8, 128), block, jnp.int32)
        for bit in range(5):
            step = 1 << bit
            ahead_of = jnp.concatenate([near[step:], near[:step]], axis=0)
            near = jnp.where(((whole & step) != 0)[None], ahead_of, near)
        next_ = jnp.concatenate([near[2:], near[:2]], axis=0)
        m = lanes((256, 128)) & 63
        near, next_ = near.reshape(256, 128), next_.reshape(256, 128)
        dst[pl.ds(variant * 256, 256), :] = jnp.where(
            m + g < 64, lane_roll(near, lax.rem(128 - g, 128)), lane_roll(next_, 64 - g)
        )

    def shifts(step):
        above, below = offsets[step, up], offsets[step, j]
        second = jnp.where(pair < 4, below + offsets[step, down], -(above + offsets[step, up2]))
        return -above, below, second

    def to_windows_of(dst, step):
        for variant, shift in enumerate(shifts(step)):
            to_windows(dst, variant, shift)

    def to_columns(src, dst, ss, rs):
        def body(n, carry):
            c = lax.rem(i + n, NGX)
            copy(tile(src, c), tile(dst, field * 64 + 8 + pair), ss, rs, up, c).start()
            copy(tile(src, 32 + c), tile(dst, field * 64 + 40 + pair), ss, rs, down, c).start()
            return carry

        lax.fori_loop(0, NGX, body, 0)

        @pl.when(far)
        def _():
            def far_body(n, carry):
                c = lax.rem(i + n, NGX)
                copy(tile(src, 64 + c), tile(dst, far_slot), ss, rs, far_row, c).start()
                return carry

            lax.fori_loop(0, NGX, far_body, 0)

    def columns_sent(src, ss, rs):
        all_tiles(src, 64, ss, rs).wait_send()

        @pl.when(far)
        def _():
            all_tiles(src, 32, ss, rs).wait_send()

    def own_windows(centre, side_west, side_east, targets):
        m = lanes((128, 128)) & 63
        for f in range(2):
            at = pl.ds(128 * f, 128)
            whole = jnp.where(
                m < 16,
                lane_roll(side_west[at, :], 112),
                jnp.where(m < 48, lane_roll(centre[at, :], 16), lane_roll(side_east[at, :], 48)),
            )
            for target in targets:
                target[512 * f + 192 : 512 * f + 320, :] = whole

    def rows_of(ref, f):
        return [
            jnp.stack([ref[pl.ds(512 * f + 4 * r + k, 8, stride=64), :] for k in range(4)])
            for r in range(16)
        ]

    def put_rows(ref, f, rows):
        for r in range(16):
            for k in range(4):
                ref[pl.ds(512 * f + 4 * r + k, 8, stride=64), :] = rows[r][k]

    def sums_to_row(value, mine, dst, sems):
        mine[...] = value
        dst[i] = value

        def body(d, carry):
            q = lax.rem(i + d, NGX)
            copy(mine, dst.at[i], s2sem.at[sems], r2sem.at[sems], j, q).start()
            return carry

        lax.fori_loop(1, NGX, body, 0)

    def sums_to_col(value, mine, dst, sems):
        mine[...] = value
        dst[j] = value

        def body(d, carry):
            q = lax.rem(j + d, NGY)
            copy(mine, dst.at[j], s2sem.at[sems], r2sem.at[sems], q, i).start()
            return carry

        lax.fori_loop(1, NGY, body, 0)

    def few(ref, count, sems):
        return copy(ref.at[pl.ds(0, count)], ref.at[pl.ds(0, count)], s2sem.at[sems], r2sem.at[sems], j, near_east)

    pending = []

    barrier = pltpu.get_barrier_semaphore()

    def greet_row(d, carry):
        pl.semaphore_signal(barrier, inc=1, device_id=(j, lax.rem(i + d, NGX)), device_id_type=MESH)
        return carry

    lax.fori_loop(1, NGX, greet_row, 0)
    for d in range(1, NGY):
        pl.semaphore_signal(barrier, inc=1, device_id=(lax.rem(j + d, NGY), i), device_id_type=MESH)

    n = lanes((128, 512))
    c = lax.broadcasted_iota(jnp.int32, (128, 512), 0)
    matrix = jnp.where(c == 4 * (n & 127) + (n >> 7), 1.0, 0.0).astype(jnp.bfloat16)
    blocks = jnp.concatenate([phase[0], phase[1], velocity[0], velocity[1]], axis=0)
    split = permuted(blocks, matrix)
    for f in range(2):
        for k in range(4):
            cut = split[64 * f : 64 * f + 64, 128 * k : 128 * k + 128]
            own[pl.ds(128 * f + k, 32, stride=4), :] = cut[:32] + lane_roll(cut[32:], 64)

    pl.semaphore_wait(barrier, NGX - 1 + NGY - 1)
    to_row(own, got, ssem.at[0], rsem.at[0])
    for row in (up, down, up2, down2):
        pl.semaphore_signal(ready, inc=1, device_id=(row, i), device_id_type=MESH)
    pending.append(all_tiles(own, 31, ssem.at[0], rsem.at[0]).wait_send)
    to_sides(own, west, east, 1)
    pending.append(all_tiles(own, 32, ssem.at[1], rsem.at[1]).wait_send)
    pending.append(all_tiles(own, 32, ssem.at[2], rsem.at[2]).wait_send)
    for ref in (window, ahead, window2):
        for f in range(2):
            ref[512 * f : 512 * f + 32, :] = jnp.zeros((32, 128), jnp.float32)
            ref[512 * f + 480 : 512 * f + 512, :] = jnp.zeros((32, 128), jnp.float32)
    all_tiles(got, 31, ssem.at[0], rsem.at[0]).wait_recv()
    to_spread(got)
    to_windows_of(sent, 0)
    pl.semaphore_wait(ready, 4)
    to_columns(sent, window, ssem.at[3], rsem.at[3])
    pending.append(lambda: columns_sent(sent, ssem.at[3], rsem.at[3]))
    to_windows_of(later, 1)
    to_columns(later, ahead, ssem.at[4], rsem.at[4])
    pending.append(lambda: columns_sent(later, ssem.at[4], rsem.at[4]))
    all_tiles(west, 32, ssem.at[1], rsem.at[1]).wait_recv()
    all_tiles(east, 32, ssem.at[2], rsem.at[2]).wait_recv()
    own_windows(own, west, east, (window, ahead))
    all_tiles(window, 80, ssem.at[3], rsem.at[3]).wait_recv()

    def solve(u, v):
        r = residual_of(u, v)
        w = precondition(r)
        q = operate(w)
        z = precondition(q)
        y = operate(z)
        return w, z, packed_sums(((r, w), (w, q), (r, z), (q, z), (z, y)))

    w, z, packed = solve(rows_of(window, 0), rows_of(window, 1))
    put_rows(stage, 0, w)
    put_rows(stage, 1, z)
    for f in range(2):
        own2[128 * f : 128 * f + 128, :] = lane_roll(stage[512 * f + 192 : 512 * f + 320, :], 112)
    to_row(own2, got2, ssem.at[5], rsem.at[5])
    pending.append(all_tiles(own2, 31, ssem.at[5], rsem.at[5]).wait_send)
    sums_to_row(packed, part, sums_row, 0)
    pending.append(few(sums_row, 31, 0).wait_send)
    to_sides(own2, west2, east2, 6)
    pending.append(all_tiles(own2, 32, ssem.at[6], rsem.at[6]).wait_send)
    pending.append(all_tiles(own2, 32, ssem.at[7], rsem.at[7]).wait_send)
    all_tiles(got2, 31, ssem.at[5], rsem.at[5]).wait_recv()
    to_spread(got2)
    to_windows_of(third, 1)
    to_columns(third, window2, ssem.at[8], rsem.at[8])
    pending.append(lambda: columns_sent(third, ssem.at[8], rsem.at[8]))
    few(sums_row, 31, 0).wait_recv()
    sums_to_col(jnp.sum(sums_row[...], axis=0), part_row, sums_col, 1)
    pending.append(few(sums_col, 7, 1).wait_send)
    all_tiles(west2, 32, ssem.at[6], rsem.at[6]).wait_recv()
    all_tiles(east2, 32, ssem.at[7], rsem.at[7]).wait_recv()
    own_windows(own2, west2, east2, (window2,))
    few(sums_col, 7, 1).wait_recv()
    c1, c2 = coefficients(jnp.sum(sums_col[...], axis=0))
    all_tiles(ahead, 80, ssem.at[4], rsem.at[4]).wait_recv()
    all_tiles(window2, 80, ssem.at[8], rsem.at[8]).wait_recv()

    def moved(u, w, z, c1, c2):
        return [a + 0.5 * mixed(c1 * b + c2 * d) for a, b, d in zip(u, w, z)]

    u = moved(rows_of(ahead, 0), rows_of(window2, 0), rows_of(window2, 1), c1, c2)
    w, z, packed = solve(u, rows_of(ahead, 1))
    sums_to_row(packed, part2, sums2_row, 2)
    pending.append(few(sums2_row, 31, 2).wait_send)
    few(sums2_row, 31, 2).wait_recv()
    sums_to_col(jnp.sum(sums2_row[...], axis=0), part2_row, sums2_col, 3)
    pending.append(few(sums2_col, 7, 3).wait_send)
    few(sums2_col, 7, 3).wait_recv()
    c1, c2 = coefficients(jnp.sum(sums2_col[...], axis=0))
    put_rows(stage, 0, moved(u, w, z, c1, c2))
    flat = jnp.concatenate([stage[pl.ds(192 + k, 32, stride=4), :] for k in range(4)], axis=1)
    rho = lax.broadcasted_iota(jnp.int32, (512, 256), 0)
    col = lanes((512, 256))
    c = col & 127
    back = ((rho >> 7) == (c & 3)) & ((rho & 127) == (col >> 7) * 64 + 16 + (c >> 2))
    flat = permuted(flat, jnp.where(back, 1.0, 0.0).astype(jnp.bfloat16))
    out[0] = flat[:, :128]
    out[1] = flat[:, 128:]

    for wait in pending:
        wait()


def local(phase, velocity, offsets):
    f32 = jnp.float32
    tiles = lambda count: pltpu.VMEM((8 * count, 128), f32)
    line, lines = pltpu.VMEM((1, 128), f32), lambda n: pltpu.VMEM((n, 1, 128), f32)
    vmem = pl.BlockSpec(memory_space=pltpu.VMEM)
    return pl.pallas_call(
        kernel,
        out_shape=jax.ShapeDtypeStruct(phase.shape, f32),
        in_specs=[pl.BlockSpec(memory_space=pltpu.SMEM), vmem, vmem],
        out_specs=vmem,
        scratch_shapes=[
            tiles(32), tiles(32), tiles(32), tiles(32), tiles(32), tiles(96), tiles(96), tiles(96), tiles(128), tiles(128), tiles(128),
            tiles(32), tiles(32), tiles(32), tiles(32), tiles(128),
            line, line, lines(32), lines(8), line, line, lines(32), lines(8),
            pltpu.SemaphoreType.DMA((9,)), pltpu.SemaphoreType.DMA((9,)),
            pltpu.SemaphoreType.DMA((4,)), pltpu.SemaphoreType.DMA((4,)), pltpu.SemaphoreType.REGULAR,
        ],
        compiler_params=pltpu.CompilerParams(collective_id=0, has_side_effects=True),
    )(offsets, phase, velocity)


def solution(mesh):
    return jax.shard_map(
        local,
        mesh=mesh,
        in_specs=(P(None, "gy", "gx"), P(None, "gy", "gx"), P()),
        out_specs=P(None, "gy", "gx"),
        check_vma=False,
    )
```

```python
import jax
import jax.numpy as jnp
from jax import lax
from jax.experimental import pallas as pl
from jax.experimental.pallas import tpu as pltpu
from jax.sharding import PartitionSpec as P

MESH = pl.DeviceIdType.MESH
NGY, NGX = 8, 32
RELAX, DIFFUSION, REACTION, ADVECTION = 0.8, 4.0, 0.5, 0.5
COUPLING = [DIFFUSION / 4.0**level for level in range(3)]
DIAGONAL = [1.0 + 4.0 * c + 2.0 for c in COUPLING]
SCALE = [RELAX / d for d in DIAGONAL]
COARSE = 4


def lanes(shape=(8, 128)):
    return lax.broadcasted_iota(jnp.int32, shape, len(shape) - 1)


def lane_roll(v, shift):
    return pltpu.roll(v, shift, 1)


def right_of(v):
    last = lane_roll(v[0], 127)[None]
    return last if v.shape[0] == 1 else jnp.concatenate([v[1:], last], axis=0)


def left_of(v):
    first = lane_roll(v[v.shape[0] - 1], 1)[None]
    return first if v.shape[0] == 1 else jnp.concatenate([first, v[:-1]], axis=0)


def sub_roll(v, shift):
    return jnp.stack([pltpu.roll(v[k], shift, 0) for k in range(v.shape[0])])


def vertical(rows):
    count = len(rows)
    after = rows[1:] + [sub_roll(rows[0], 7)]
    before = [sub_roll(rows[count - 1], 1)] + rows[:-1]
    return [a + b for a, b in zip(after, before)]


def beside(rows):
    return [s + (right_of(v) + left_of(v)) for s, v in zip(vertical(rows), rows)]


def coarser(rows):
    out = []
    for r in range(0, len(rows), 2):
        s = rows[r] + rows[r + 1]
        out.append(0.25 * jnp.stack([s[k] + s[k + 1] for k in range(0, s.shape[0], 2)]))
    return out


def finer(rows):
    out = []
    for v in rows:
        wide = jnp.stack([v[k // 2] for k in range(2 * v.shape[0])])
        out += [wide, wide]
    return out


def of_planes(total, difference):
    return jnp.where(lanes() < 64, jnp.float32(total), jnp.float32(difference))


def mixed(v):
    other = jnp.stack([lane_roll(v[k], 64) for k in range(v.shape[0])])
    return jnp.where((lanes() < 64)[None], v + other, other - v)


def operate(rows):
    d = of_planes(DIAGONAL[0] - 2.0, DIAGONAL[0] + 2.0)
    return [d * v - COUPLING[0] * b for v, b in zip(rows, beside(rows))]


def smoothing(level):
    d, s = DIAGONAL[level], SCALE[level]
    return s, of_planes(1.0 - s * (d - 2.0), 1.0 - s * (d + 2.0)), s * COUPLING[level]


def precondition(rows, level=0):
    scale, keep, spread = smoothing(level)
    if level == 2:
        base = [scale * v for v in rows]
        e = base
        for _ in range(COARSE - 1):
            e = [f + keep * v + spread * b for f, v, b in zip(base, e, beside(e))]
        return e
    defect = [keep * v + spread * b for v, b in zip(rows, beside(rows))]
    correction = finer(precondition(coarser(defect), level + 1))
    e = [scale * v + c for v, c in zip(rows, correction)]
    return [scale * f + keep * v + spread * b for f, v, b in zip(rows, e, beside(e))]


def residual_of(u, v):
    out = []
    for s, f, speed in zip(vertical(u), u, v):
        east, west = right_of(f), left_of(f)
        around = s + (east + west)
        source = f + REACTION * (f - f * f * f) - ADVECTION * speed * (east - west)
        other = jnp.stack([lane_roll(f[k], 64) for k in range(4)])
        applied = DIAGONAL[0] * f - COUPLING[0] * around - 2.0 * other
        out.append(mixed(source - applied))
    return out


def own_sum(first, second):
    total = None
    for a, b in zip(first, second):
        product = a * b
        part = (product[0] + product[1]) + (product[2] + product[3])
        total = part if total is None else total + part
    m = lanes() & 63
    total = jnp.where((m >= 16) & (m < 48), total, 0.0)
    return total[3:4] + total[4:5]


def packed_sums(pairs):
    sums = [own_sum(a, b) for a, b in pairs]
    tile = jnp.concatenate(sums + [jnp.zeros((8 - len(sums), 128), jnp.float32)], axis=0)
    for shift in (64, 32, 16):
        tile = tile + lane_roll(tile, shift)
    row = lax.broadcasted_iota(jnp.int32, (8, 128), 0)
    return jnp.sum(jnp.where((lanes() >> 4) == row, tile, 0.0), axis=0, keepdims=True)


def coefficients(packed):
    group = lanes((1, 128)) >> 4
    rw, wq, rz, qz, zy = (
        jnp.sum(jnp.where(group == d, packed, 0.0), axis=1, keepdims=True) for d in range(5)
    )
    a0 = rw / wq
    following = a0 * (a0 * qz - rz)
    b = 1.0 + following / rw
    a1 = following / (b * b * wq - 2.0 * b * a0 * qz + a0 * a0 * zy)
    return a0 + a1 * b, -a1 * a0


def permuted(x, matrix):
    n = x.shape[0]
    high = x.astype(jnp.bfloat16)
    rest = x - high.astype(jnp.float32)
    mid = rest.astype(jnp.bfloat16)
    low = (rest - mid.astype(jnp.float32)).astype(jnp.bfloat16)
    y = jnp.dot(jnp.concatenate([high, mid, low], axis=0), matrix, preferred_element_type=jnp.float32)
    return (y[:n] + y[n : 2 * n]) + y[2 * n :]


def held_by(device):
    return lax.rem(device, 4) * 4 + device // 8


def kernel(
    offsets, phase, velocity, out,
    own, got, spread, west, east, sent, later, third, window, ahead, stage,
    own2, got2, west2, east2, window2, flat_rows,
    part, part_row, sums_row, sums_col, part2, part2_row, sums2_row, sums2_col,
    ssem, rsem, s2sem, r2sem, ready,
):
    j, i = lax.axis_index("gy"), lax.axis_index("gx")
    chip_x, chip_z = i // 8, lax.rem(i, 8)
    pair = held_by(i)
    up, down = lax.rem(j + 1, NGY), lax.rem(j + NGY - 1, NGY)
    up2, down2 = lax.rem(j + 2, NGY), lax.rem(j + NGY - 2, NGY)
    far = (pair < 4) | (pair >= 12)
    far_row = jnp.where(pair < 4, down2, up2)
    far_slot = jnp.where(pair < 4, 56 + pair, pair - 8)
    near_west, near_east = lax.rem(i + NGX - 1, NGX), lax.rem(i + 1, NGX)

    def tile(ref, slot, count=1):
        return ref.at[pl.ds(pl.multiple_of(slot * 8, 8), 8 * count)]

    def copy(src, dst, ss, rs, row, column):
        return pltpu.make_async_remote_copy(
            src_ref=src, dst_ref=dst, send_sem=ss, recv_sem=rs, device_id=(row, column), device_id_type=MESH
        )

    def to_row(src, dst, ss, rs):
        def body(d, carry):
            q = lax.rem(i + d, NGX)
            copy(tile(src, held_by(q)), tile(dst, i), ss, rs, j, q).start()
            return carry

        lax.fori_loop(1, NGX, body, 0)
        dst[pl.ds(pl.multiple_of(i * 8, 8), 8), :] = src[pl.ds(pl.multiple_of(pair * 8, 8), 8), :]

    def to_sides(src, dst_west, dst_east, sems):
        copy(src, dst_west, ssem.at[sems], rsem.at[sems], j, near_east).start()
        copy(src, dst_east, ssem.at[sems + 1], rsem.at[sems + 1], j, near_west).start()

    def all_tiles(ref, count, ss, rs):
        return copy(ref.at[pl.ds(0, 8 * count)], ref.at[pl.ds(0, 8 * count)], ss, rs, j, near_east)

    def to_spread(src):
        here = src[...]
        following = jnp.concatenate([here[8:], here[:8]], axis=0)
        m = lanes((256, 128)) & 63
        spread[0:256, :] = jnp.where(m < 32, here, lane_roll(following, 32))
        spread[256:512, :] = jnp.where(m < 32, lane_roll(here, 96), following)

    def to_windows(dst, variant, shift):
        start = lax.rem(shift // 4 + (4096 - 16), 1024)
        block, g = start // 32, lax.rem(start, 32)
        whole = jnp.full((8, 128), block, jnp.int32)
        m = lanes((256, 128)) & 63
        for f in range(2):
            near = spread[256 * f : 256 * f + 256, :].reshape(32, 8, 128)
            for bit in range(5):
                step = 1 << bit
                ahead_of = jnp.concatenate([near[step:], near[:step]], axis=0)
                near = jnp.where(((whole & step) != 0)[None], ahead_of, near)
            next_ = jnp.concatenate([near[2:], near[:2]], axis=0)
            near, next_ = near.reshape(256, 128), next_.reshape(256, 128)
            moved_on = jnp.where(
                m + g < 64, lane_roll(near, lax.rem(128 - g, 128)), lane_roll(next_, 64 - g)
            )
            for c in range(NGX):
                at = 16 * (32 * variant + c) + 8 * f
                dst[at : at + 8, :] = moved_on[8 * c : 8 * c + 8]

    def shifts(step):
        above, below = offsets[step, up], offsets[step, j]
        second = jnp.where(pair < 4, below + offsets[step, down], -(above + offsets[step, up2]))
        return -above, below, second

    def to_windows_of(dst, step):
        for variant, shift in enumerate(shifts(step)):
            to_windows(dst, variant, shift)

    def both_fields(ref, slot, count=1):
        return ref.at[pl.ds(pl.multiple_of(slot * 16, 16), 16 * count)]

    def to_columns(src, dst, ss, rs):
        def served(n):
            return lax.rem(chip_x + n // 4, 4) * 8 + lax.rem(chip_z + 6 + lax.rem(n, 4), 8)

        def body(n, carry):
            c = served(n)
            copy(both_fields(src, c), both_fields(dst, 8 + pair), ss, rs, up, c).start()
            copy(both_fields(src, 32 + c), both_fields(dst, 40 + pair), ss, rs, down, c).start()
            return carry

        lax.fori_loop(0, 16, body, 0)

        @pl.when(far)
        def _():
            def far_body(n, carry):
                c = served(n)
                copy(both_fields(src, 64 + c), both_fields(dst, far_slot), ss, rs, far_row, c).start()
                return carry

            lax.fori_loop(0, 16, far_body, 0)

    def columns_sent(src, ss, rs):
        all_tiles(src, 64, ss, rs).wait_send()

        @pl.when(far)
        def _():
            all_tiles(src, 32, ss, rs).wait_send()

    def own_windows(centre, side_west, side_east, targets):
        m = lanes((128, 128)) & 63
        for f, turns in enumerate(((112, 16, 48), (80, 112, 16))):
            whole = jnp.where(
                m < 16,
                lane_roll(side_west[...], turns[0]),
                jnp.where(m < 48, lane_roll(centre[...], turns[1]), lane_roll(side_east[...], turns[2])),
            )
            for target in targets:
                for p in range(16):
                    at = 16 * (24 + p) + 8 * f
                    target[at : at + 8, :] = whole[8 * p : 8 * p + 8]

    def row_at(f, r, k):
        return pl.ds(16 * (r // 2) + 8 * f + 4 * (r % 2) + k, 8, stride=128)

    def rows_of(ref, f):
        return [jnp.stack([ref[row_at(f, r, k), :] for k in range(4)]) for r in range(16)]

    def put_rows(ref, f, rows):
        for r in range(16):
            for k in range(4):
                ref[row_at(f, r, k), :] = rows[r][k]

    def sums_to_row(value, mine, dst, sems):
        mine[...] = value
        dst[i] = value

        def body(d, carry):
            q = lax.rem(i + d, NGX)
            copy(mine, dst.at[i], s2sem.at[sems], r2sem.at[sems], j, q).start()
            return carry

        lax.fori_loop(1, NGX, body, 0)

    def sums_to_col(value, mine, dst, sems):
        mine[...] = value
        dst[j] = value

        def body(d, carry):
            q = lax.rem(j + d, NGY)
            copy(mine, dst.at[j], s2sem.at[sems], r2sem.at[sems], q, i).start()
            return carry

        lax.fori_loop(1, NGY, body, 0)

    def few(ref, count, sems):
        return copy(ref.at[pl.ds(0, count)], ref.at[pl.ds(0, count)], s2sem.at[sems], r2sem.at[sems], j, near_east)

    pending = []

    barrier = pltpu.get_barrier_semaphore()

    def greet_row(d, carry):
        pl.semaphore_signal(barrier, inc=1, device_id=(j, lax.rem(i + d, NGX)), device_id_type=MESH)
        return carry

    lax.fori_loop(1, NGX, greet_row, 0)
    for d in range(1, NGY):
        pl.semaphore_signal(barrier, inc=1, device_id=(lax.rem(j + d, NGY), i), device_id_type=MESH)

    n = lanes((128, 512))
    c = lax.broadcasted_iota(jnp.int32, (128, 512), 0)
    matrix = jnp.where(c == 4 * (n & 127) + (n >> 7), 1.0, 0.0).astype(jnp.bfloat16)
    blocks = jnp.concatenate([phase[0], phase[1], velocity[0], velocity[1]], axis=0)
    split = permuted(blocks, matrix)
    for k in range(4):
        u, v = (split[64 * f : 64 * f + 64, 128 * k : 128 * k + 128] for f in range(2))
        u, v = (cut[:32] + lane_roll(cut[32:], 64) for cut in (u, v))
        own[pl.ds(k, 32, stride=4), :] = u + lane_roll(v, 32)

    pl.semaphore_wait(barrier, NGX - 1 + NGY - 1)
    to_row(own, got, ssem.at[0], rsem.at[0])
    for row in (up, down, up2, down2):
        pl.semaphore_signal(ready, inc=1, device_id=(row, i), device_id_type=MESH)
    pending.append(all_tiles(got, 31, ssem.at[0], rsem.at[0]).wait_send)
    to_sides(own, west, east, 1)
    pending.append(all_tiles(own, 16, ssem.at[1], rsem.at[1]).wait_send)
    pending.append(all_tiles(own, 16, ssem.at[2], rsem.at[2]).wait_send)
    for ref in (window, ahead, window2):
        ref[0:64, :] = jnp.zeros((64, 128), jnp.float32)
        ref[960:1024, :] = jnp.zeros((64, 128), jnp.float32)
    all_tiles(got, 31, ssem.at[0], rsem.at[0]).wait_recv()
    to_spread(got)
    to_windows_of(sent, 0)
    pl.semaphore_wait(ready, 4)
    to_columns(sent, window, ssem.at[3], rsem.at[3])
    pending.append(lambda: columns_sent(sent, ssem.at[3], rsem.at[3]))
    to_windows_of(later, 1)
    to_columns(later, ahead, ssem.at[4], rsem.at[4])
    pending.append(lambda: columns_sent(later, ssem.at[4], rsem.at[4]))
    all_tiles(west, 16, ssem.at[1], rsem.at[1]).wait_recv()
    all_tiles(east, 16, ssem.at[2], rsem.at[2]).wait_recv()
    own_windows(own, west, east, (window, ahead))
    all_tiles(window, 80, ssem.at[3], rsem.at[3]).wait_recv()

    def solve(u, v):
        r = residual_of(u, v)
        w = precondition(r)
        q = operate(w)
        z = precondition(q)
        y = operate(z)
        return w, z, packed_sums(((r, w), (w, q), (r, z), (q, z), (z, y)))

    w, z, packed = solve(rows_of(window, 0), rows_of(window, 1))
    put_rows(stage, 0, w)
    put_rows(stage, 1, z)
    m = lanes() & 63
    for p in range(16):
        at = 16 * (24 + p)
        own2[8 * p : 8 * p + 8, :] = jnp.where(
            m < 32, lane_roll(stage[at : at + 8, :], 112), lane_roll(stage[at + 8 : at + 16, :], 16)
        )
    to_row(own2, got2, ssem.at[5], rsem.at[5])
    pending.append(all_tiles(got2, 31, ssem.at[5], rsem.at[5]).wait_send)
    sums_to_row(packed, part, sums_row, 0)
    pending.append(few(sums_row, 31, 0).wait_send)
    to_sides(own2, west2, east2, 6)
    pending.append(all_tiles(own2, 16, ssem.at[6], rsem.at[6]).wait_send)
    pending.append(all_tiles(own2, 16, ssem.at[7], rsem.at[7]).wait_send)
    all_tiles(got2, 31, ssem.at[5], rsem.at[5]).wait_recv()
    to_spread(got2)
    to_windows_of(third, 1)
    to_columns(third, window2, ssem.at[8], rsem.at[8])
    pending.append(lambda: columns_sent(third, ssem.at[8], rsem.at[8]))
    few(sums_row, 31, 0).wait_recv()
    sums_to_col(jnp.sum(sums_row[...], axis=0), part_row, sums_col, 1)
    pending.append(few(sums_col, 7, 1).wait_send)
    all_tiles(west2, 16, ssem.at[6], rsem.at[6]).wait_recv()
    all_tiles(east2, 16, ssem.at[7], rsem.at[7]).wait_recv()
    own_windows(own2, west2, east2, (window2,))
    few(sums_col, 7, 1).wait_recv()
    c1, c2 = coefficients(jnp.sum(sums_col[...], axis=0))
    all_tiles(ahead, 80, ssem.at[4], rsem.at[4]).wait_recv()
    all_tiles(window2, 80, ssem.at[8], rsem.at[8]).wait_recv()

    def moved(u, w, z, c1, c2):
        return [a + 0.5 * mixed(c1 * b + c2 * d) for a, b, d in zip(u, w, z)]

    u = moved(rows_of(ahead, 0), rows_of(window2, 0), rows_of(window2, 1), c1, c2)
    w, z, packed = solve(u, rows_of(ahead, 1))
    sums_to_row(packed, part2, sums2_row, 2)
    pending.append(few(sums2_row, 31, 2).wait_send)
    few(sums2_row, 31, 2).wait_recv()
    sums_to_col(jnp.sum(sums2_row[...], axis=0), part2_row, sums2_col, 3)
    pending.append(few(sums2_col, 7, 3).wait_send)
    few(sums2_col, 7, 3).wait_recv()
    c1, c2 = coefficients(jnp.sum(sums2_col[...], axis=0))
    put_rows(stage, 0, moved(u, w, z, c1, c2))
    block = [stage[16 * (24 + p) : 16 * (24 + p) + 8, :] for p in range(16)]
    flat_rows[...] = jnp.concatenate(block, axis=0)
    flat = jnp.concatenate([flat_rows[pl.ds(k, 32, stride=4), :] for k in range(4)], axis=1)
    rho = lax.broadcasted_iota(jnp.int32, (512, 256), 0)
    col = lanes((512, 256))
    c = col & 127
    back = ((rho >> 7) == (c & 3)) & ((rho & 127) == (col >> 7) * 64 + 16 + (c >> 2))
    flat = permuted(flat, jnp.where(back, 1.0, 0.0).astype(jnp.bfloat16))
    out[0] = flat[:, :128]
    out[1] = flat[:, 128:]

    for wait in pending:
        wait()


def local(phase, velocity, offsets):
    f32 = jnp.float32
    tiles = lambda count: pltpu.VMEM((8 * count, 128), f32)
    line, lines = pltpu.VMEM((1, 128), f32), lambda n: pltpu.VMEM((n, 1, 128), f32)
    vmem = pl.BlockSpec(memory_space=pltpu.VMEM)
    return pl.pallas_call(
        kernel,
        out_shape=jax.ShapeDtypeStruct(phase.shape, f32),
        in_specs=[pl.BlockSpec(memory_space=pltpu.SMEM), vmem, vmem],
        out_specs=vmem,
        scratch_shapes=[
            tiles(16), tiles(32), tiles(64), tiles(16), tiles(16), tiles(192), tiles(192), tiles(192), tiles(128), tiles(128), tiles(128),
            tiles(16), tiles(32), tiles(16), tiles(16), tiles(128), tiles(16),
            line, line, lines(32), lines(8), line, line, lines(32), lines(8),
            pltpu.SemaphoreType.DMA((9,)), pltpu.SemaphoreType.DMA((9,)),
            pltpu.SemaphoreType.DMA((4,)), pltpu.SemaphoreType.DMA((4,)), pltpu.SemaphoreType.REGULAR,
        ],
        compiler_params=pltpu.CompilerParams(collective_id=0, has_side_effects=True),
    )(offsets, phase, velocity)


def solution(mesh):
    return jax.shard_map(
        local,
        mesh=mesh,
        in_specs=(P(None, "gy", "gx"), P(None, "gy", "gx"), P()),
        out_specs=P(None, "gy", "gx"),
        check_vma=False,
    )
```

```python
import jax
import jax.numpy as jnp
from jax import lax
from jax.experimental import pallas as pl
from jax.experimental.pallas import tpu as pltpu
from jax.sharding import PartitionSpec as P

MESH = pl.DeviceIdType.MESH
NGY, NGX = 8, 32
RELAX, DIFFUSION, REACTION, ADVECTION = 0.8, 4.0, 0.5, 0.5
COUPLING = [DIFFUSION / 4.0**level for level in range(3)]
DIAGONAL = [1.0 + 4.0 * c + 2.0 for c in COUPLING]
SCALE = [RELAX / d for d in DIAGONAL]
COARSE = 4


def lanes(shape=(8, 128)):
    return lax.broadcasted_iota(jnp.int32, shape, len(shape) - 1)


def lane_roll(v, shift):
    return pltpu.roll(v, shift, 1)


def right_of(v):
    last = lane_roll(v[0], 127)[None]
    return last if v.shape[0] == 1 else jnp.concatenate([v[1:], last], axis=0)


def left_of(v):
    first = lane_roll(v[v.shape[0] - 1], 1)[None]
    return first if v.shape[0] == 1 else jnp.concatenate([first, v[:-1]], axis=0)


def sub_roll(v, shift):
    return jnp.stack([pltpu.roll(v[k], shift, 0) for k in range(v.shape[0])])


def vertical(rows):
    count = len(rows)
    after = rows[1:] + [sub_roll(rows[0], 7)]
    before = [sub_roll(rows[count - 1], 1)] + rows[:-1]
    return [a + b for a, b in zip(after, before)]


def beside(rows):
    return [s + (right_of(v) + left_of(v)) for s, v in zip(vertical(rows), rows)]


def coarser(rows):
    out = []
    for r in range(0, len(rows), 2):
        s = rows[r] + rows[r + 1]
        out.append(0.25 * jnp.stack([s[k] + s[k + 1] for k in range(0, s.shape[0], 2)]))
    return out


def finer(rows):
    out = []
    for v in rows:
        wide = jnp.stack([v[k // 2] for k in range(2 * v.shape[0])])
        out += [wide, wide]
    return out


def of_planes(total, difference):
    return jnp.where(lanes() < 64, jnp.float32(total), jnp.float32(difference))


def mixed(v):
    other = jnp.stack([lane_roll(v[k], 64) for k in range(v.shape[0])])
    return jnp.where((lanes() < 64)[None], v + other, other - v)


def operate(rows):
    d = of_planes(DIAGONAL[0] - 2.0, DIAGONAL[0] + 2.0)
    return [d * v - COUPLING[0] * b for v, b in zip(rows, beside(rows))]


def smoothing(level):
    d, s = DIAGONAL[level], SCALE[level]
    return s, of_planes(1.0 - s * (d - 2.0), 1.0 - s * (d + 2.0)), s * COUPLING[level]


def precondition(rows, level=0):
    scale, keep, spread = smoothing(level)
    if level == 2:
        base = [scale * v for v in rows]
        e = base
        for _ in range(COARSE - 1):
            e = [f + keep * v + spread * b for f, v, b in zip(base, e, beside(e))]
        return e
    defect = [keep * v + spread * b for v, b in zip(rows, beside(rows))]
    correction = finer(precondition(coarser(defect), level + 1))
    e = [scale * v + c for v, c in zip(rows, correction)]
    return [scale * f + keep * v + spread * b for f, v, b in zip(rows, e, beside(e))]


def residual_of(u, v):
    out = []
    for s, f, speed in zip(vertical(u), u, v):
        east, west = right_of(f), left_of(f)
        around = s + (east + west)
        source = f + REACTION * (f - f * f * f) - ADVECTION * speed * (east - west)
        other = jnp.stack([lane_roll(f[k], 64) for k in range(4)])
        applied = DIAGONAL[0] * f - COUPLING[0] * around - 2.0 * other
        out.append(mixed(source - applied))
    return out


def own_sum(first, second):
    total = None
    for a, b in zip(first, second):
        product = a * b
        part = (product[0] + product[1]) + (product[2] + product[3])
        total = part if total is None else total + part
    m = lanes() & 63
    total = jnp.where((m >= 16) & (m < 48), total, 0.0)
    return total[3:4] + total[4:5]


def packed_sums(pairs):
    sums = [own_sum(a, b) for a, b in pairs]
    tile = jnp.concatenate(sums + [jnp.zeros((8 - len(sums), 128), jnp.float32)], axis=0)
    for shift in (64, 32, 16):
        tile = tile + lane_roll(tile, shift)
    row = lax.broadcasted_iota(jnp.int32, (8, 128), 0)
    return jnp.sum(jnp.where((lanes() >> 4) == row, tile, 0.0), axis=0, keepdims=True)


def coefficients(packed):
    group = lanes((1, 128)) >> 4
    rw, wq, rz, qz, zy = (
        jnp.sum(jnp.where(group == d, packed, 0.0), axis=1, keepdims=True) for d in range(5)
    )
    a0 = rw / wq
    following = a0 * (a0 * qz - rz)
    b = 1.0 + following / rw
    a1 = following / (b * b * wq - 2.0 * b * a0 * qz + a0 * a0 * zy)
    return a0 + a1 * b, -a1 * a0


def permuted(x, matrix):
    n = x.shape[0]
    high = x.astype(jnp.bfloat16)
    rest = x - high.astype(jnp.float32)
    mid = rest.astype(jnp.bfloat16)
    low = (rest - mid.astype(jnp.float32)).astype(jnp.bfloat16)
    y = jnp.dot(jnp.concatenate([high, mid, low], axis=0), matrix, preferred_element_type=jnp.float32)
    return (y[:n] + y[n : 2 * n]) + y[2 * n :]


def held_by(device):
    return lax.rem(device, 4) * 4 + device // 8


def kernel(
    offsets, phase, velocity, out,
    own, got, spread, west, east, sent, later, third, window, ahead, stage,
    own2, got2, west2, east2, window2, flat_rows,
    part, part_row, sums_row, sums_col, part2, part2_chip, sums2_core, sums2,
    ssem, rsem, s2sem, r2sem, ready,
):
    j, i = lax.axis_index("gy"), lax.axis_index("gx")
    chip_x, chip_z = i // 8, lax.rem(i, 8)
    pair = held_by(i)
    up, down = lax.rem(j + 1, NGY), lax.rem(j + NGY - 1, NGY)
    up2, down2 = lax.rem(j + 2, NGY), lax.rem(j + NGY - 2, NGY)
    far = (pair < 4) | (pair >= 12)
    far_row = jnp.where(pair < 4, down2, up2)
    far_slot = jnp.where(pair < 4, 56 + pair, pair - 8)
    near_west, near_east = lax.rem(i + NGX - 1, NGX), lax.rem(i + 1, NGX)

    def tile(ref, slot, count=1):
        return ref.at[pl.ds(pl.multiple_of(slot * 8, 8), 8 * count)]

    def copy(src, dst, ss, rs, row, column):
        return pltpu.make_async_remote_copy(
            src_ref=src, dst_ref=dst, send_sem=ss, recv_sem=rs, device_id=(row, column), device_id_type=MESH
        )

    def to_row(src, dst, ss, rs):
        def body(d, carry):
            q = lax.rem(i + d, NGX)
            copy(tile(src, held_by(q)), tile(dst, i), ss, rs, j, q).start()
            return carry

        lax.fori_loop(1, NGX, body, 0)
        dst[pl.ds(pl.multiple_of(i * 8, 8), 8), :] = src[pl.ds(pl.multiple_of(pair * 8, 8), 8), :]

    def to_sides(src, dst_west, dst_east, sems):
        copy(src, dst_west, ssem.at[sems], rsem.at[sems], j, near_east).start()
        copy(src, dst_east, ssem.at[sems + 1], rsem.at[sems + 1], j, near_west).start()

    def all_tiles(ref, count, ss, rs):
        return copy(ref.at[pl.ds(0, 8 * count)], ref.at[pl.ds(0, 8 * count)], ss, rs, j, near_east)

    def to_spread(src):
        here = src[...]
        following = jnp.concatenate([here[8:], here[:8]], axis=0)
        m = lanes((256, 128)) & 63
        spread[0:256, :] = jnp.where(m < 32, here, lane_roll(following, 32))
        spread[256:512, :] = jnp.where(m < 32, lane_roll(here, 96), following)

    def to_windows(dst, variant, shift):
        start = lax.rem(shift // 4 + (4096 - 16), 1024)
        block, g = start // 32, lax.rem(start, 32)
        whole = jnp.full((8, 128), block, jnp.int32)
        m = lanes((256, 128)) & 63
        for f in range(2):
            near = spread[256 * f : 256 * f + 256, :].reshape(32, 8, 128)
            for bit in range(5):
                step = 1 << bit
                ahead_of = jnp.concatenate([near[step:], near[:step]], axis=0)
                near = jnp.where(((whole & step) != 0)[None], ahead_of, near)
            next_ = jnp.concatenate([near[2:], near[:2]], axis=0)
            near, next_ = near.reshape(256, 128), next_.reshape(256, 128)
            moved_on = jnp.where(
                m + g < 64, lane_roll(near, lax.rem(128 - g, 128)), lane_roll(next_, 64 - g)
            )
            for c in range(NGX):
                at = 16 * (32 * variant + c) + 8 * f
                dst[at : at + 8, :] = moved_on[8 * c : 8 * c + 8]

    def shifts(step):
        above, below = offsets[step, up], offsets[step, j]
        second = jnp.where(pair < 4, below + offsets[step, down], -(above + offsets[step, up2]))
        return -above, below, second

    def both_fields(ref, slot, count=1):
        return ref.at[pl.ds(pl.multiple_of(slot * 16, 16), 16 * count)]

    def to_columns(src, dst, step, ss, rs):
        near_by, opposite, second = shifts(step)

        def send(variant, slot, row):
            def body(n, carry):
                c = lax.rem(chip_x + lax.rem(n, 4), 4) * 8 + lax.rem(chip_z + 6 + n // 4, 8)
                copy(both_fields(src, 32 * variant + c), both_fields(dst, slot), ss, rs, row, c).start()
                return carry

            lax.fori_loop(0, 16, body, 0)

        to_windows(src, 2, second)
        pl.when(far)(lambda: send(2, far_slot, far_row))
        to_windows(src, 0, near_by)
        send(0, 8 + pair, up)
        to_windows(src, 1, opposite)
        send(1, 40 + pair, down)

    def columns_sent(src, ss, rs):
        all_tiles(src, 64, ss, rs).wait_send()

        @pl.when(far)
        def _():
            all_tiles(src, 32, ss, rs).wait_send()

    def own_windows(centre, side_west, side_east, targets):
        m = lanes((128, 128)) & 63
        for f, turns in enumerate(((112, 16, 48), (80, 112, 16))):
            whole = jnp.where(
                m < 16,
                lane_roll(side_west[...], turns[0]),
                jnp.where(m < 48, lane_roll(centre[...], turns[1]), lane_roll(side_east[...], turns[2])),
            )
            for target in targets:
                for p in range(16):
                    at = 16 * (24 + p) + 8 * f
                    target[at : at + 8, :] = whole[8 * p : 8 * p + 8]

    def row_at(f, r, k):
        return pl.ds(16 * (r // 2) + 8 * f + 4 * (r % 2) + k, 8, stride=128)

    def rows_of(ref, f):
        return [jnp.stack([ref[row_at(f, r, k), :] for k in range(4)]) for r in range(16)]

    def put_rows(ref, f, rows):
        for r in range(16):
            for k in range(4):
                ref[row_at(f, r, k), :] = rows[r][k]

    def sums_to_row(value, mine, dst, sems):
        mine[...] = value
        dst[i] = value

        def body(d, carry):
            q = lax.rem(i + d, NGX)
            copy(mine, dst.at[i], s2sem.at[sems], r2sem.at[sems], j, q).start()
            return carry

        lax.fori_loop(1, NGX, body, 0)

    def sums_to_col(value, mine, dst, sems):
        mine[...] = value
        dst[j] = value

        def body(d, carry):
            q = lax.rem(j + d, NGY)
            copy(mine, dst.at[j], s2sem.at[sems], r2sem.at[sems], q, i).start()
            return carry

        lax.fori_loop(1, NGY, body, 0)

    def few(ref, count, sems):
        return copy(ref.at[pl.ds(0, count)], ref.at[pl.ds(0, count)], s2sem.at[sems], r2sem.at[sems], j, near_east)

    pending = []

    barrier = pltpu.get_barrier_semaphore()

    def greet_row(d, carry):
        pl.semaphore_signal(barrier, inc=1, device_id=(j, lax.rem(i + d, NGX)), device_id_type=MESH)
        return carry

    lax.fori_loop(1, NGX, greet_row, 0)
    for d in range(1, NGY):
        pl.semaphore_signal(barrier, inc=1, device_id=(lax.rem(j + d, NGY), i), device_id_type=MESH)

    n = lanes((128, 512))
    c = lax.broadcasted_iota(jnp.int32, (128, 512), 0)
    matrix = jnp.where(c == 4 * (n & 127) + (n >> 7), 1.0, 0.0).astype(jnp.bfloat16)
    blocks = jnp.concatenate([phase[0], phase[1], velocity[0], velocity[1]], axis=0)
    split = permuted(blocks, matrix)
    for k in range(4):
        u, v = (split[64 * f : 64 * f + 64, 128 * k : 128 * k + 128] for f in range(2))
        u, v = (cut[:32] + lane_roll(cut[32:], 64) for cut in (u, v))
        own[pl.ds(k, 32, stride=4), :] = u + lane_roll(v, 32)

    pl.semaphore_wait(barrier, NGX - 1 + NGY - 1)
    to_row(own, got, ssem.at[0], rsem.at[0])
    for row in (up, down, up2, down2):
        pl.semaphore_signal(ready, inc=1, device_id=(row, i), device_id_type=MESH)
    pending.append(all_tiles(got, 31, ssem.at[0], rsem.at[0]).wait_send)
    to_sides(own, west, east, 1)
    pending.append(all_tiles(own, 16, ssem.at[1], rsem.at[1]).wait_send)
    pending.append(all_tiles(own, 16, ssem.at[2], rsem.at[2]).wait_send)
    for ref in (window, ahead, window2):
        ref[0:64, :] = jnp.zeros((64, 128), jnp.float32)
        ref[960:1024, :] = jnp.zeros((64, 128), jnp.float32)
    all_tiles(got, 31, ssem.at[0], rsem.at[0]).wait_recv()
    to_spread(got)
    pl.semaphore_wait(ready, 4)
    to_columns(sent, window, 0, ssem.at[3], rsem.at[3])
    pending.append(lambda: columns_sent(sent, ssem.at[3], rsem.at[3]))
    to_columns(later, ahead, 1, ssem.at[4], rsem.at[4])
    pending.append(lambda: columns_sent(later, ssem.at[4], rsem.at[4]))
    all_tiles(west, 16, ssem.at[1], rsem.at[1]).wait_recv()
    all_tiles(east, 16, ssem.at[2], rsem.at[2]).wait_recv()
    own_windows(own, west, east, (window, ahead))
    all_tiles(window, 80, ssem.at[3], rsem.at[3]).wait_recv()

    def solve(u, v):
        r = residual_of(u, v)
        w = precondition(r)
        q = operate(w)
        z = precondition(q)
        y = operate(z)
        return w, z, packed_sums(((r, w), (w, q), (r, z), (q, z), (z, y)))

    w, z, packed = solve(rows_of(window, 0), rows_of(window, 1))
    put_rows(stage, 0, w)
    put_rows(stage, 1, z)
    m = lanes() & 63
    for p in range(16):
        at = 16 * (24 + p)
        own2[8 * p : 8 * p + 8, :] = jnp.where(
            m < 32, lane_roll(stage[at : at + 8, :], 112), lane_roll(stage[at + 8 : at + 16, :], 16)
        )
    to_row(own2, got2, ssem.at[5], rsem.at[5])
    pending.append(all_tiles(got2, 31, ssem.at[5], rsem.at[5]).wait_send)
    sums_to_row(packed, part, sums_row, 0)
    pending.append(few(sums_row, 31, 0).wait_send)
    to_sides(own2, west2, east2, 6)
    pending.append(all_tiles(own2, 16, ssem.at[6], rsem.at[6]).wait_send)
    pending.append(all_tiles(own2, 16, ssem.at[7], rsem.at[7]).wait_send)
    all_tiles(got2, 31, ssem.at[5], rsem.at[5]).wait_recv()
    to_spread(got2)
    to_columns(third, window2, 1, ssem.at[8], rsem.at[8])
    pending.append(lambda: columns_sent(third, ssem.at[8], rsem.at[8]))
    few(sums_row, 31, 0).wait_recv()
    sums_to_col(jnp.sum(sums_row[...], axis=0), part_row, sums_col, 1)
    pending.append(few(sums_col, 7, 1).wait_send)
    all_tiles(west2, 16, ssem.at[6], rsem.at[6]).wait_recv()
    all_tiles(east2, 16, ssem.at[7], rsem.at[7]).wait_recv()
    own_windows(own2, west2, east2, (window2,))
    few(sums_col, 7, 1).wait_recv()
    c1, c2 = coefficients(jnp.sum(sums_col[...], axis=0))
    all_tiles(ahead, 80, ssem.at[4], rsem.at[4]).wait_recv()
    all_tiles(window2, 80, ssem.at[8], rsem.at[8]).wait_recv()

    def moved(u, w, z, c1, c2):
        return [a + 0.5 * mixed(c1 * b + c2 * d) for a, b, d in zip(u, w, z)]

    u = moved(rows_of(ahead, 0), rows_of(window2, 0), rows_of(window2, 1), c1, c2)
    w, z, packed = solve(u, rows_of(ahead, 1))
    part2[...] = packed
    to_core = copy(part2, sums2_core, s2sem.at[2], r2sem.at[2], j + 1 - 2 * lax.rem(j, 2), i)
    to_core.start()
    pending.append(to_core.wait_send)
    put_rows(stage, 0, u)
    put_rows(window, 0, w)
    put_rows(window, 1, z)
    to_core.wait_recv()
    total = packed + sums2_core[...]
    part2_chip[...] = total
    chip_y = j // 2
    sums2[chip_y * NGX + i] = total

    def to_chips(n, carry):
        y, c = lax.rem(chip_y + n // NGX, 4), lax.rem(i + n, NGX)
        copy(part2_chip, sums2.at[chip_y * NGX + i], s2sem.at[3], r2sem.at[3], 2 * y + lax.rem(j, 2), c).start()
        return carry

    lax.fori_loop(1, 128, to_chips, 0)
    pending.append(few(sums2, 127, 3).wait_send)
    for f, (ref, at_f) in enumerate(((stage, 0), (window, 0), (window, 1))):
        for p in range(16):
            at = 16 * (24 + p) + 8 * at_f
            flat_rows[128 * f + 8 * p : 128 * f + 8 * p + 8, :] = ref[at : at + 8, :]
    flat = jnp.concatenate([flat_rows[pl.ds(k, 96, stride=4), :] for k in range(4)], axis=1)
    rho = lax.broadcasted_iota(jnp.int32, (512, 256), 0)
    col = lanes((512, 256))
    c = col & 127
    same = ((rho >> 7) == (c & 3)) & ((rho & 63) == 16 + (c >> 2))
    plane, of_plane = (rho >> 6) & 1, col >> 7
    straight = jnp.where(same & (plane == of_plane), 1.0, 0.0).astype(jnp.bfloat16)
    halves = jnp.where(same, jnp.where(plane + of_plane == 2, -0.5, 0.5), 0.0).astype(jnp.bfloat16)
    u = permuted(flat[:32], straight)
    wz = permuted(flat[32:], halves)
    few(sums2, 127, 3).wait_recv()
    c1, c2 = coefficients(jnp.sum(sums2[...], axis=0))
    flat = u + c1 * wz[:32] + c2 * wz[32:]
    out[0] = flat[:, :128]
    out[1] = flat[:, 128:]

    for wait in pending:
        wait()


def local(phase, velocity, offsets):
    f32 = jnp.float32
    tiles = lambda count: pltpu.VMEM((8 * count, 128), f32)
    line, lines = pltpu.VMEM((1, 128), f32), lambda n: pltpu.VMEM((n, 1, 128), f32)
    vmem = pl.BlockSpec(memory_space=pltpu.VMEM)
    return pl.pallas_call(
        kernel,
        out_shape=jax.ShapeDtypeStruct(phase.shape, f32),
        in_specs=[pl.BlockSpec(memory_space=pltpu.SMEM), vmem, vmem],
        out_specs=vmem,
        scratch_shapes=[
            tiles(16), tiles(32), tiles(64), tiles(16), tiles(16), tiles(192), tiles(192), tiles(192), tiles(128), tiles(128), tiles(128),
            tiles(16), tiles(32), tiles(16), tiles(16), tiles(128), tiles(48),
            line, line, lines(32), lines(8), line, line, line, lines(128),
            pltpu.SemaphoreType.DMA((9,)), pltpu.SemaphoreType.DMA((9,)),
            pltpu.SemaphoreType.DMA((4,)), pltpu.SemaphoreType.DMA((4,)), pltpu.SemaphoreType.REGULAR,
        ],
        compiler_params=pltpu.CompilerParams(collective_id=0, has_side_effects=True),
    )(offsets, phase, velocity)


def solution(mesh):
    return jax.shard_map(
        local,
        mesh=mesh,
        in_specs=(P(None, "gy", "gx"), P(None, "gy", "gx"), P()),
        out_specs=P(None, "gy", "gx"),
        check_vma=False,
    )
```

```python
import jax
import jax.numpy as jnp
from jax import lax
from jax.experimental import pallas as pl
from jax.experimental.pallas import tpu as pltpu
from jax.sharding import PartitionSpec as P

MESH = pl.DeviceIdType.MESH
NGY, NGX = 8, 32
RELAX, DIFFUSION, REACTION, ADVECTION = 0.8, 4.0, 0.5, 0.5
COUPLING = [DIFFUSION / 4.0**level for level in range(3)]
DIAGONAL = [1.0 + 4.0 * c + 2.0 for c in COUPLING]
SCALE = [RELAX / d for d in DIAGONAL]
COARSE = 4


def lanes(shape=(8, 128)):
    return lax.broadcasted_iota(jnp.int32, shape, len(shape) - 1)


def lane_roll(v, shift):
    return pltpu.roll(v, shift, 1)


def right_of(v):
    last = lane_roll(v[0], 127)[None]
    return last if v.shape[0] == 1 else jnp.concatenate([v[1:], last], axis=0)


def left_of(v):
    first = lane_roll(v[v.shape[0] - 1], 1)[None]
    return first if v.shape[0] == 1 else jnp.concatenate([first, v[:-1]], axis=0)


def sub_roll(v, shift):
    return jnp.stack([pltpu.roll(v[k], shift, 0) for k in range(v.shape[0])])


def vertical(rows):
    count = len(rows)
    after = rows[1:] + [sub_roll(rows[0], 7)]
    before = [sub_roll(rows[count - 1], 1)] + rows[:-1]
    return [a + b for a, b in zip(after, before)]


def beside(rows):
    return [s + (right_of(v) + left_of(v)) for s, v in zip(vertical(rows), rows)]


def coarser(rows):
    out = []
    for r in range(0, len(rows), 2):
        s = rows[r] + rows[r + 1]
        out.append(0.25 * jnp.stack([s[k] + s[k + 1] for k in range(0, s.shape[0], 2)]))
    return out


def finer(rows):
    out = []
    for v in rows:
        wide = jnp.stack([v[k // 2] for k in range(2 * v.shape[0])])
        out += [wide, wide]
    return out


def of_planes(total, difference):
    return jnp.where(lanes() < 64, jnp.float32(total), jnp.float32(difference))


def mixed(v):
    other = jnp.stack([lane_roll(v[k], 64) for k in range(v.shape[0])])
    return jnp.where((lanes() < 64)[None], v + other, other - v)


def operate(rows):
    d = of_planes(DIAGONAL[0] - 2.0, DIAGONAL[0] + 2.0)
    return [d * v - COUPLING[0] * b for v, b in zip(rows, beside(rows))]


def smoothing(level):
    d, s = DIAGONAL[level], SCALE[level]
    return s, of_planes(1.0 - s * (d - 2.0), 1.0 - s * (d + 2.0)), s * COUPLING[level]


def precondition(rows, level=0):
    scale, keep, spread = smoothing(level)
    if level == 2:
        base = [scale * v for v in rows]
        e = base
        for _ in range(COARSE - 1):
            e = [f + keep * v + spread * b for f, v, b in zip(base, e, beside(e))]
        return e
    defect = [keep * v + spread * b for v, b in zip(rows, beside(rows))]
    correction = finer(precondition(coarser(defect), level + 1))
    e = [scale * v + c for v, c in zip(rows, correction)]
    return [scale * f + keep * v + spread * b for f, v, b in zip(rows, e, beside(e))]


def residual_of(u, v):
    out = []
    for s, f, speed in zip(vertical(u), u, v):
        east, west = right_of(f), left_of(f)
        around = s + (east + west)
        source = f + REACTION * (f - f * f * f) - ADVECTION * speed * (east - west)
        other = jnp.stack([lane_roll(f[k], 64) for k in range(4)])
        applied = DIAGONAL[0] * f - COUPLING[0] * around - 2.0 * other
        out.append(mixed(source - applied))
    return out


def own_sum(first, second):
    total = None
    for a, b in zip(first, second):
        product = a * b
        part = (product[0] + product[1]) + (product[2] + product[3])
        total = part if total is None else total + part
    m = lanes() & 63
    total = jnp.where((m >= 16) & (m < 48), total, 0.0)
    return total[3:4] + total[4:5]


def packed_sums(pairs):
    sums = [own_sum(a, b) for a, b in pairs]
    tile = jnp.concatenate(sums + [jnp.zeros((8 - len(sums), 128), jnp.float32)], axis=0)
    for shift in (64, 32, 16):
        tile = tile + lane_roll(tile, shift)
    row = lax.broadcasted_iota(jnp.int32, (8, 128), 0)
    return jnp.sum(jnp.where((lanes() >> 4) == row, tile, 0.0), axis=0, keepdims=True)


def coefficients(packed):
    group = lanes((1, 128)) >> 4
    rw, wq, rz, qz, zy = (
        jnp.sum(jnp.where(group == d, packed, 0.0), axis=1, keepdims=True) for d in range(5)
    )
    a0 = rw / wq
    following = a0 * (a0 * qz - rz)
    b = 1.0 + following / rw
    a1 = following / (b * b * wq - 2.0 * b * a0 * qz + a0 * a0 * zy)
    return a0 + a1 * b, -a1 * a0


def permuted(x, matrix):
    n = x.shape[0]
    high = x.astype(jnp.bfloat16)
    rest = x - high.astype(jnp.float32)
    mid = rest.astype(jnp.bfloat16)
    low = (rest - mid.astype(jnp.float32)).astype(jnp.bfloat16)
    y = jnp.dot(jnp.concatenate([high, mid, low], axis=0), matrix, preferred_element_type=jnp.float32)
    return (y[:n] + y[n : 2 * n]) + y[2 * n :]


def held_by(device):
    return lax.rem(device, 4) * 4 + device // 8


def kernel(
    offsets, phase, velocity, out,
    own, got, spread, west, east, sent, later, third, window, ahead, stage,
    own2, got2, west2, east2, window2,
    part, part_row, sums_row, sums_col, part2, part2_chip, sums2_core, sums2,
    ssem, rsem, s2sem, r2sem, ready,
):
    j, i = lax.axis_index("gy"), lax.axis_index("gx")
    chip_x, chip_z = i // 8, lax.rem(i, 8)
    pair = held_by(i)
    up, down = lax.rem(j + 1, NGY), lax.rem(j + NGY - 1, NGY)
    up2, down2 = lax.rem(j + 2, NGY), lax.rem(j + NGY - 2, NGY)
    first_half = pair < 8
    far_row = jnp.where(first_half, down2, up2)
    far_tile = jnp.where(first_half, 112 + 2 * pair, 2 * pair - 15)
    far_from = jnp.where(first_half, 0, 1)
    near_west, near_east = lax.rem(i + NGX - 1, NGX), lax.rem(i + 1, NGX)

    def tile(ref, slot, count=1):
        return ref.at[pl.ds(pl.multiple_of(slot * 8, 8), 8 * count)]

    def copy(src, dst, ss, rs, row, column):
        return pltpu.make_async_remote_copy(
            src_ref=src, dst_ref=dst, send_sem=ss, recv_sem=rs, device_id=(row, column), device_id_type=MESH
        )

    def to_row(src, dst, ss, rs):
        def body(d, carry):
            q = lax.rem(i + d, NGX)
            copy(tile(src, held_by(q)), tile(dst, i), ss, rs, j, q).start()
            return carry

        lax.fori_loop(1, NGX, body, 0)
        dst[pl.ds(pl.multiple_of(i * 8, 8), 8), :] = src[pl.ds(pl.multiple_of(pair * 8, 8), 8), :]

    def to_sides(src, dst_west, dst_east, sems):
        copy(src, dst_west, ssem.at[sems], rsem.at[sems], j, near_east).start()
        copy(src, dst_east, ssem.at[sems + 1], rsem.at[sems + 1], j, near_west).start()

    def all_tiles(ref, count, ss, rs):
        return copy(ref.at[pl.ds(0, 8 * count)], ref.at[pl.ds(0, 8 * count)], ss, rs, j, near_east)

    def by_row(first, second):
        count = first.shape[0]
        top = (lax.broadcasted_iota(jnp.int32, first.shape, 0) & 7) < 4
        return (
            jnp.where(top, first, pltpu.roll(second, 4, 0)),
            jnp.where(top, pltpu.roll(first, count - 4, 0), second),
        )

    def to_spread(src):
        here = src[...]
        following = jnp.concatenate([here[8:], here[:8]], axis=0)
        m = lanes((256, 128)) & 63
        first = jnp.where(m < 32, here, lane_roll(following, 32))
        second = jnp.where(m < 32, lane_roll(here, 96), following)
        spread[0:256, :], spread[256:512, :] = by_row(first, second)

    def to_windows(dst, variant, shift):
        start = lax.rem(shift // 4 + (4096 - 16), 1024)
        block, g = start // 32, lax.rem(start, 32)
        whole = jnp.full((8, 128), block, jnp.int32)
        m = lanes((256, 128)) & 63
        for f in range(2):
            near = spread[256 * f : 256 * f + 256, :].reshape(32, 8, 128)
            for bit in range(5):
                step = 1 << bit
                ahead_of = jnp.concatenate([near[step:], near[:step]], axis=0)
                near = jnp.where(((whole & step) != 0)[None], ahead_of, near)
            next_ = jnp.concatenate([near[2:], near[:2]], axis=0)
            near, next_ = near.reshape(256, 128), next_.reshape(256, 128)
            moved_on = jnp.where(
                m + g < 64, lane_roll(near, lax.rem(128 - g, 128)), lane_roll(next_, 64 - g)
            )
            for c in range(NGX):
                at = 16 * (32 * variant + c) + 8 * f
                dst[at : at + 8, :] = moved_on[8 * c : 8 * c + 8]

    def shifts(step):
        above, below = offsets[step, up], offsets[step, j]
        second = jnp.where(first_half, below + offsets[step, down], -(above + offsets[step, up2]))
        return -above, below, second

    def both_fields(ref, slot, count=1):
        return ref.at[pl.ds(pl.multiple_of(slot * 16, 16), 16 * count)]

    def to_columns(src, dst, step, ss, rs):
        near_by, opposite, second = shifts(step)

        def served(n):
            return lax.rem(chip_x + lax.rem(n, 4), 4) * 8 + lax.rem(chip_z + 6 + n // 4, 8)

        def send(variant, slot, row):
            def body(n, carry):
                c = served(n)
                copy(both_fields(src, 32 * variant + c), both_fields(dst, slot), ss, rs, row, c).start()
                return carry

            lax.fori_loop(0, 16, body, 0)

        to_windows(src, 2, second)

        def far_body(n, carry):
            c = served(n)
            copy(tile(src, 2 * (64 + c) + far_from), tile(dst, far_tile), ss, rs, far_row, c).start()
            return carry

        lax.fori_loop(0, 16, far_body, 0)
        to_windows(src, 0, near_by)
        send(0, 8 + pair, up)
        to_windows(src, 1, opposite)
        send(1, 40 + pair, down)

    def columns_sent(src, ss, rs):
        all_tiles(src, 80, ss, rs).wait_send()

    def own_windows(centre, side_west, side_east, targets):
        m = lanes((128, 128)) & 63
        fields = (
            jnp.where(
                m < 16,
                lane_roll(side_west[...], turns[0]),
                jnp.where(m < 48, lane_roll(centre[...], turns[1]), lane_roll(side_east[...], turns[2])),
            )
            for turns in ((112, 16, 48), (80, 112, 16))
        )
        for h, whole in enumerate(by_row(*fields)):
            for target in targets:
                for p in range(16):
                    at = 16 * (24 + p) + 8 * h
                    target[at : at + 8, :] = whole[8 * p : 8 * p + 8]

    def row_at(f, r, k):
        return pl.ds(16 * (r % 8) + 8 * (r // 8) + 4 * f + k, 8, stride=128)

    def rows_of(ref, f):
        return [jnp.stack([ref[row_at(f, r, k), :] for k in range(4)]) for r in range(16)]

    def put_rows(ref, f, rows):
        for r in range(16):
            for k in range(4):
                ref[row_at(f, r, k), :] = rows[r][k]

    def sums_to_row(value, mine, dst, sems):
        mine[...] = value
        dst[i] = value

        def body(d, carry):
            q = lax.rem(i + d, NGX)
            copy(mine, dst.at[i], s2sem.at[sems], r2sem.at[sems], j, q).start()
            return carry

        lax.fori_loop(1, NGX, body, 0)

    def sums_to_col(value, mine, dst, sems):
        mine[...] = value
        dst[j] = value

        def body(d, carry):
            q = lax.rem(j + d, NGY)
            copy(mine, dst.at[j], s2sem.at[sems], r2sem.at[sems], q, i).start()
            return carry

        lax.fori_loop(1, NGY, body, 0)

    def few(ref, count, sems):
        return copy(ref.at[pl.ds(0, count)], ref.at[pl.ds(0, count)], s2sem.at[sems], r2sem.at[sems], j, near_east)

    pending = []

    barrier = pltpu.get_barrier_semaphore()

    def greet_row(d, carry):
        pl.semaphore_signal(barrier, inc=1, device_id=(j, lax.rem(i + d, NGX)), device_id_type=MESH)
        return carry

    lax.fori_loop(1, NGX, greet_row, 0)
    for d in range(1, NGY):
        pl.semaphore_signal(barrier, inc=1, device_id=(lax.rem(j + d, NGY), i), device_id_type=MESH)

    n = lanes((128, 512))
    c = lax.broadcasted_iota(jnp.int32, (128, 512), 0)
    matrix = jnp.where(c == 4 * (n & 127) + (n >> 7), 1.0, 0.0).astype(jnp.bfloat16)
    blocks = jnp.concatenate([phase[0], phase[1], velocity[0], velocity[1]], axis=0)
    split = permuted(blocks, matrix)
    for k in range(4):
        u, v = (split[64 * f : 64 * f + 64, 128 * k : 128 * k + 128] for f in range(2))
        u, v = (cut[:32] + lane_roll(cut[32:], 64) for cut in (u, v))
        u = u + lane_roll(v, 32)
        for g in range(4):
            own[pl.ds(64 * (g // 2) + 4 * (g % 2) + k, 8, stride=8), :] = u[8 * g : 8 * g + 8]

    pl.semaphore_wait(barrier, NGX - 1 + NGY - 1)
    to_row(own, got, ssem.at[0], rsem.at[0])
    for row in (up, down, up2, down2):
        pl.semaphore_signal(ready, inc=1, device_id=(row, i), device_id_type=MESH)
    pending.append(all_tiles(got, 31, ssem.at[0], rsem.at[0]).wait_send)
    to_sides(own, west, east, 1)
    pending.append(all_tiles(own, 16, ssem.at[1], rsem.at[1]).wait_send)
    pending.append(all_tiles(own, 16, ssem.at[2], rsem.at[2]).wait_send)
    for ref in (window, ahead, window2):
        for p in range(8):
            for at in (16 * p, 16 * (56 + p) + 8):
                ref[at : at + 8, :] = jnp.zeros((8, 128), jnp.float32)
    all_tiles(got, 31, ssem.at[0], rsem.at[0]).wait_recv()
    to_spread(got)
    pl.semaphore_wait(ready, 4)
    to_columns(sent, window, 0, ssem.at[3], rsem.at[3])
    pending.append(lambda: columns_sent(sent, ssem.at[3], rsem.at[3]))
    to_columns(later, ahead, 1, ssem.at[4], rsem.at[4])
    pending.append(lambda: columns_sent(later, ssem.at[4], rsem.at[4]))
    all_tiles(west, 16, ssem.at[1], rsem.at[1]).wait_recv()
    all_tiles(east, 16, ssem.at[2], rsem.at[2]).wait_recv()
    own_windows(own, west, east, (window, ahead))
    all_tiles(window, 80, ssem.at[3], rsem.at[3]).wait_recv()

    def solve(u, v):
        r = residual_of(u, v)
        w = precondition(r)
        q = operate(w)
        z = precondition(q)
        y = operate(z)
        return w, z, packed_sums(((r, w), (w, q), (r, z), (q, z), (z, y)))

    w, z, packed = solve(rows_of(window, 0), rows_of(window, 1))
    put_rows(stage, 0, w)
    put_rows(stage, 1, z)
    m = lanes() & 63
    for p in range(16):
        at = 16 * (24 + p)
        first, second = by_row(stage[at : at + 8, :], stage[at + 8 : at + 16, :])
        own2[8 * p : 8 * p + 8, :] = jnp.where(m < 32, lane_roll(first, 112), lane_roll(second, 16))
    to_row(own2, got2, ssem.at[5], rsem.at[5])
    pending.append(all_tiles(got2, 31, ssem.at[5], rsem.at[5]).wait_send)
    sums_to_row(packed, part, sums_row, 0)
    pending.append(few(sums_row, 31, 0).wait_send)
    to_sides(own2, west2, east2, 6)
    pending.append(all_tiles(own2, 16, ssem.at[6], rsem.at[6]).wait_send)
    pending.append(all_tiles(own2, 16, ssem.at[7], rsem.at[7]).wait_send)
    all_tiles(got2, 31, ssem.at[5], rsem.at[5]).wait_recv()
    to_spread(got2)
    to_columns(third, window2, 1, ssem.at[8], rsem.at[8])
    pending.append(lambda: columns_sent(third, ssem.at[8], rsem.at[8]))
    few(sums_row, 31, 0).wait_recv()
    sums_to_col(jnp.sum(sums_row[...], axis=0), part_row, sums_col, 1)
    pending.append(few(sums_col, 7, 1).wait_send)
    all_tiles(west2, 16, ssem.at[6], rsem.at[6]).wait_recv()
    all_tiles(east2, 16, ssem.at[7], rsem.at[7]).wait_recv()
    own_windows(own2, west2, east2, (window2,))
    few(sums_col, 7, 1).wait_recv()
    c1, c2 = coefficients(jnp.sum(sums_col[...], axis=0))
    all_tiles(ahead, 80, ssem.at[4], rsem.at[4]).wait_recv()
    all_tiles(window2, 80, ssem.at[8], rsem.at[8]).wait_recv()

    def moved(u, w, z, c1, c2):
        return [a + 0.5 * mixed(c1 * b + c2 * d) for a, b, d in zip(u, w, z)]

    u = moved(rows_of(ahead, 0), rows_of(window2, 0), rows_of(window2, 1), c1, c2)
    w, z, packed = solve(u, rows_of(ahead, 1))
    part2[...] = packed
    to_core = copy(part2, sums2_core, s2sem.at[2], r2sem.at[2], j + 1 - 2 * lax.rem(j, 2), i)
    to_core.start()
    pending.append(to_core.wait_send)
    put_rows(stage, 0, u)
    put_rows(window, 0, w)
    put_rows(window, 1, z)
    to_core.wait_recv()
    total = packed + sums2_core[...]
    part2_chip[...] = total
    chip_y = j // 2
    sums2[chip_y * NGX + i] = total

    def to_chips(n, carry):
        y, c = lax.rem(chip_y + n // NGX, 4), lax.rem(i + n, NGX)
        copy(part2_chip, sums2.at[chip_y * NGX + i], s2sem.at[3], r2sem.at[3], 2 * y + lax.rem(j, 2), c).start()
        return carry

    lax.fori_loop(1, 128, to_chips, 0)
    pending.append(few(sums2, 127, 3).wait_send)
    flat = jnp.concatenate(
        [
            jnp.concatenate(
                [
                    ref[pl.ds(16 * (24 + 8 * (g // 2)) + 8 * (g % 2) + 4 * f + k, 8, stride=16), :]
                    for ref, f in ((stage, 0), (window, 0), (window, 1))
                    for g in range(4)
                ],
                axis=0,
            )
            for k in range(4)
        ],
        axis=1,
    )
    rho = lax.broadcasted_iota(jnp.int32, (512, 256), 0)
    col = lanes((512, 256))
    c = col & 127
    same = ((rho >> 7) == (c & 3)) & ((rho & 63) == 16 + (c >> 2))
    plane, of_plane = (rho >> 6) & 1, col >> 7
    straight = jnp.where(same & (plane == of_plane), 1.0, 0.0).astype(jnp.bfloat16)
    halves = jnp.where(same, jnp.where(plane + of_plane == 2, -0.5, 0.5), 0.0).astype(jnp.bfloat16)
    u = permuted(flat[:32], straight)
    wz = permuted(flat[32:], halves)
    few(sums2, 127, 3).wait_recv()
    c1, c2 = coefficients(jnp.sum(sums2[...], axis=0))
    flat = u + c1 * wz[:32] + c2 * wz[32:]
    out[0] = flat[:, :128]
    out[1] = flat[:, 128:]

    for wait in pending:
        wait()


def local(phase, velocity, offsets):
    f32 = jnp.float32
    tiles = lambda count: pltpu.VMEM((8 * count, 128), f32)
    line, lines = pltpu.VMEM((1, 128), f32), lambda n: pltpu.VMEM((n, 1, 128), f32)
    vmem = pl.BlockSpec(memory_space=pltpu.VMEM)
    return pl.pallas_call(
        kernel,
        out_shape=jax.ShapeDtypeStruct(phase.shape, f32),
        in_specs=[pl.BlockSpec(memory_space=pltpu.SMEM), vmem, vmem],
        out_specs=vmem,
        scratch_shapes=[
            tiles(16), tiles(32), tiles(64), tiles(16), tiles(16), tiles(192), tiles(192), tiles(192), tiles(128), tiles(128), tiles(128),
            tiles(16), tiles(32), tiles(16), tiles(16), tiles(128),
            line, line, lines(32), lines(8), line, line, line, lines(128),
            pltpu.SemaphoreType.DMA((9,)), pltpu.SemaphoreType.DMA((9,)),
            pltpu.SemaphoreType.DMA((4,)), pltpu.SemaphoreType.DMA((4,)), pltpu.SemaphoreType.REGULAR,
        ],
        compiler_params=pltpu.CompilerParams(collective_id=0, has_side_effects=True),
    )(offsets, phase, velocity)


def solution(mesh):
    return jax.shard_map(
        local,
        mesh=mesh,
        in_specs=(P(None, "gy", "gx"), P(None, "gy", "gx"), P()),
        out_specs=P(None, "gy", "gx"),
        check_vma=False,
    )
```

```python
import jax
import jax.numpy as jnp
from jax import lax
from jax.experimental import pallas as pl
from jax.experimental.pallas import tpu as pltpu
from jax.sharding import PartitionSpec as P

MESH = pl.DeviceIdType.MESH
NGY, NGX = 8, 32
RELAX, DIFFUSION, REACTION, ADVECTION = 0.8, 4.0, 0.5, 0.5
COUPLING = [DIFFUSION / 4.0**level for level in range(3)]
DIAGONAL = [1.0 + 4.0 * c + 2.0 for c in COUPLING]
SCALE = [RELAX / d for d in DIAGONAL]
COARSE = 4


def lanes(shape=(8, 128)):
    return lax.broadcasted_iota(jnp.int32, shape, len(shape) - 1)


def lane_roll(v, shift):
    return pltpu.roll(v, shift, 1)


def right_of(v):
    last = lane_roll(v[0], 127)[None]
    return last if v.shape[0] == 1 else jnp.concatenate([v[1:], last], axis=0)


def left_of(v):
    first = lane_roll(v[v.shape[0] - 1], 1)[None]
    return first if v.shape[0] == 1 else jnp.concatenate([first, v[:-1]], axis=0)


def sub_roll(v, shift):
    return jnp.stack([pltpu.roll(v[k], shift, 0) for k in range(v.shape[0])])


def vertical(rows):
    count = len(rows)
    after = rows[1:] + [sub_roll(rows[0], 7)]
    before = [sub_roll(rows[count - 1], 1)] + rows[:-1]
    return [a + b for a, b in zip(after, before)]


def beside(rows):
    return [s + (right_of(v) + left_of(v)) for s, v in zip(vertical(rows), rows)]


def coarser(rows):
    out = []
    for r in range(0, len(rows), 2):
        s = rows[r] + rows[r + 1]
        out.append(0.25 * jnp.stack([s[k] + s[k + 1] for k in range(0, s.shape[0], 2)]))
    return out


def finer(rows):
    out = []
    for v in rows:
        wide = jnp.stack([v[k // 2] for k in range(2 * v.shape[0])])
        out += [wide, wide]
    return out


def of_planes(total, difference):
    return jnp.where(lanes() < 64, jnp.float32(total), jnp.float32(difference))


def mixed(v):
    other = jnp.stack([lane_roll(v[k], 64) for k in range(v.shape[0])])
    return jnp.where((lanes() < 64)[None], v + other, other - v)


def operate(rows):
    d = of_planes(DIAGONAL[0] - 2.0, DIAGONAL[0] + 2.0)
    return [d * v - COUPLING[0] * b for v, b in zip(rows, beside(rows))]


def smoothing(level):
    d, s = DIAGONAL[level], SCALE[level]
    return s, of_planes(1.0 - s * (d - 2.0), 1.0 - s * (d + 2.0)), s * COUPLING[level]


def precondition(rows, level=0):
    scale, keep, spread = smoothing(level)
    if level == 2:
        base = [scale * v for v in rows]
        e = base
        for _ in range(COARSE - 1):
            e = [f + keep * v + spread * b for f, v, b in zip(base, e, beside(e))]
        return e
    defect = [keep * v + spread * b for v, b in zip(rows, beside(rows))]
    correction = finer(precondition(coarser(defect), level + 1))
    e = [scale * v + c for v, c in zip(rows, correction)]
    return [scale * f + keep * v + spread * b for f, v, b in zip(rows, e, beside(e))]


def residual_of(u, v):
    out = []
    for s, f, speed in zip(vertical(u), u, v):
        east, west = right_of(f), left_of(f)
        around = s + (east + west)
        source = f + REACTION * (f - f * f * f) - ADVECTION * speed * (east - west)
        other = jnp.stack([lane_roll(f[k], 64) for k in range(4)])
        applied = DIAGONAL[0] * f - COUPLING[0] * around - 2.0 * other
        out.append(mixed(source - applied))
    return out


def own_sum(first, second):
    total = None
    for a, b in zip(first, second):
        product = a * b
        part = (product[0] + product[1]) + (product[2] + product[3])
        total = part if total is None else total + part
    m = lanes() & 63
    total = jnp.where((m >= 16) & (m < 48), total, 0.0)
    return total[3:4] + total[4:5]


def packed_sums(pairs):
    sums = [own_sum(a, b) for a, b in pairs]
    tile = jnp.concatenate(sums + [jnp.zeros((8 - len(sums), 128), jnp.float32)], axis=0)
    for shift in (64, 32, 16):
        tile = tile + lane_roll(tile, shift)
    row = lax.broadcasted_iota(jnp.int32, (8, 128), 0)
    return jnp.sum(jnp.where((lanes() >> 4) == row, tile, 0.0), axis=0, keepdims=True)


def coefficients(packed):
    group = lanes((1, 128)) >> 4
    rw, wq, rz, qz, zy = (
        jnp.sum(jnp.where(group == d, packed, 0.0), axis=1, keepdims=True) for d in range(5)
    )
    a0 = rw / wq
    following = a0 * (a0 * qz - rz)
    b = 1.0 + following / rw
    a1 = following / (b * b * wq - 2.0 * b * a0 * qz + a0 * a0 * zy)
    return a0 + a1 * b, -a1 * a0


def permuted(x, matrix):
    n = x.shape[0]
    high = x.astype(jnp.bfloat16)
    rest = x - high.astype(jnp.float32)
    mid = rest.astype(jnp.bfloat16)
    low = (rest - mid.astype(jnp.float32)).astype(jnp.bfloat16)
    y = jnp.dot(jnp.concatenate([high, mid, low], axis=0), matrix, preferred_element_type=jnp.float32)
    return (y[:n] + y[n : 2 * n]) + y[2 * n :]


def held_by(device):
    return lax.rem(device, 4) * 4 + device // 8


def kernel(
    offsets, phase, velocity, out,
    own, got, spread, west, east, sent, later, third, window, ahead, stage,
    own2, got2, west2, east2, window2,
    part, part_row, sums_row, sums_col, part2, part2_chip, sums2_core, sums2,
    ssem, rsem, s2sem, r2sem, ready,
):
    j, i = lax.axis_index("gy"), lax.axis_index("gx")
    chip_x, chip_z = i // 8, lax.rem(i, 8)
    pair = held_by(i)
    up, down = lax.rem(j + 1, NGY), lax.rem(j + NGY - 1, NGY)
    up2, down2 = lax.rem(j + 2, NGY), lax.rem(j + NGY - 2, NGY)
    first_half = pair < 8
    far_row = jnp.where(first_half, down2, up2)
    far_tile = jnp.where(first_half, 112 + 2 * pair, 2 * pair - 15)
    far_from = jnp.where(first_half, 0, 1)
    near_west, near_east = lax.rem(i + NGX - 1, NGX), lax.rem(i + 1, NGX)

    def tile(ref, slot, count=1):
        return ref.at[pl.ds(pl.multiple_of(slot * 8, 8), 8 * count)]

    def copy(src, dst, ss, rs, row, column):
        return pltpu.make_async_remote_copy(
            src_ref=src, dst_ref=dst, send_sem=ss, recv_sem=rs, device_id=(row, column), device_id_type=MESH
        )

    def to_row(src, dst, ss, rs):
        def body(d, carry):
            q = lax.rem(i + d, NGX)
            copy(tile(src, held_by(q)), tile(dst, i), ss, rs, j, q).start()
            return carry

        lax.fori_loop(1, NGX, body, 0)
        dst[pl.ds(pl.multiple_of(i * 8, 8), 8), :] = src[pl.ds(pl.multiple_of(pair * 8, 8), 8), :]

    def to_sides(src, dst_west, dst_east, sems):
        copy(src, dst_west, ssem.at[sems], rsem.at[sems], j, near_east).start()
        copy(src, dst_east, ssem.at[sems + 1], rsem.at[sems + 1], j, near_west).start()

    def all_tiles(ref, count, ss, rs):
        return copy(ref.at[pl.ds(0, 8 * count)], ref.at[pl.ds(0, 8 * count)], ss, rs, j, near_east)

    def by_row(first, second):
        count = first.shape[0]
        top = (lax.broadcasted_iota(jnp.int32, first.shape, 0) & 7) < 4
        return (
            jnp.where(top, first, pltpu.roll(second, 4, 0)),
            jnp.where(top, pltpu.roll(first, count - 4, 0), second),
        )

    def to_spread(src):
        here = src[...]
        following = jnp.concatenate([here[8:], here[:8]], axis=0)
        m = lanes((256, 128)) & 63
        first = jnp.where(m < 32, here, lane_roll(following, 32))
        second = jnp.where(m < 32, lane_roll(here, 96), following)
        spread[0:256, :], spread[256:512, :] = by_row(first, second)

    def to_windows(dst, variant, shift, parts=(0, 256)):
        start = lax.rem(shift // 4 + (4096 - 16), 1024)
        block, g = start // 32, lax.rem(start, 32)
        whole = jnp.full((8, 128), block, jnp.int32)
        m = lanes((256, 128)) & 63
        for h, part_at in enumerate(parts):
            near = spread[pl.ds(part_at, 256), :].reshape(32, 8, 128)
            for bit in range(5):
                step = 1 << bit
                ahead_of = jnp.concatenate([near[step:], near[:step]], axis=0)
                near = jnp.where(((whole & step) != 0)[None], ahead_of, near)
            next_ = jnp.concatenate([near[2:], near[:2]], axis=0)
            near, next_ = near.reshape(256, 128), next_.reshape(256, 128)
            moved_on = jnp.where(
                m + g < 64, lane_roll(near, lax.rem(128 - g, 128)), lane_roll(next_, 64 - g)
            )
            for c in range(NGX):
                at = 16 * (32 * variant + c) + 8 * h
                dst[at : at + 8, :] = moved_on[8 * c : 8 * c + 8]

    def shifts(step):
        above, below = offsets[step, up], offsets[step, j]
        second = jnp.where(first_half, below + offsets[step, down], -(above + offsets[step, up2]))
        return -above, below, second

    def both_fields(ref, slot, count=1):
        return ref.at[pl.ds(pl.multiple_of(slot * 16, 16), 16 * count)]

    def to_columns(src, dst, step, ss, rs):
        near_by, opposite, second = shifts(step)

        def served(n):
            return lax.rem(chip_x + lax.rem(n, 4), 4) * 8 + lax.rem(chip_z + 6 + n // 4, 8)

        def send(variant, slot, row):
            def body(n, carry):
                c = served(n)
                copy(both_fields(src, 32 * variant + c), both_fields(dst, slot), ss, rs, row, c).start()
                return carry

            lax.fori_loop(0, 16, body, 0)

        to_windows(src, 2, second, (pl.multiple_of(far_from * 256, 256),))

        def far_body(n, carry):
            c = served(n)
            copy(tile(src, 2 * (64 + c)), tile(dst, far_tile), ss, rs, far_row, c).start()
            return carry

        lax.fori_loop(0, 16, far_body, 0)
        to_windows(src, 0, near_by)
        send(0, 8 + pair, up)
        to_windows(src, 1, opposite)
        send(1, 40 + pair, down)

    def columns_sent(src, ss, rs):
        all_tiles(src, 80, ss, rs).wait_send()

    def own_windows(centre, side_west, side_east, targets):
        m = lanes((128, 128)) & 63
        fields = (
            jnp.where(
                m < 16,
                lane_roll(side_west[...], turns[0]),
                jnp.where(m < 48, lane_roll(centre[...], turns[1]), lane_roll(side_east[...], turns[2])),
            )
            for turns in ((112, 16, 48), (80, 112, 16))
        )
        for h, whole in enumerate(by_row(*fields)):
            for target in targets:
                for p in range(16):
                    at = 16 * (24 + p) + 8 * h
                    target[at : at + 8, :] = whole[8 * p : 8 * p + 8]

    def row_at(f, r, k):
        return pl.ds(16 * (r % 8) + 8 * (r // 8) + 4 * f + k, 8, stride=128)

    def rows_of(ref, f):
        return [jnp.stack([ref[row_at(f, r, k), :] for k in range(4)]) for r in range(16)]

    def put_rows(ref, f, rows):
        for r in range(16):
            for k in range(4):
                ref[row_at(f, r, k), :] = rows[r][k]

    def sums_to_row(value, mine, dst, sems):
        mine[...] = value
        dst[i] = value

        def body(d, carry):
            q = lax.rem(i + d, NGX)
            copy(mine, dst.at[i], s2sem.at[sems], r2sem.at[sems], j, q).start()
            return carry

        lax.fori_loop(1, NGX, body, 0)

    def sums_to_col(value, mine, dst, sems):
        mine[...] = value
        dst[j] = value

        def body(d, carry):
            q = lax.rem(j + d, NGY)
            copy(mine, dst.at[j], s2sem.at[sems], r2sem.at[sems], q, i).start()
            return carry

        lax.fori_loop(1, NGY, body, 0)

    def few(ref, count, sems):
        return copy(ref.at[pl.ds(0, count)], ref.at[pl.ds(0, count)], s2sem.at[sems], r2sem.at[sems], j, near_east)

    pending = []

    barrier = pltpu.get_barrier_semaphore()

    def greet_row(d, carry):
        pl.semaphore_signal(barrier, inc=1, device_id=(j, lax.rem(i + d, NGX)), device_id_type=MESH)
        return carry

    lax.fori_loop(1, NGX, greet_row, 0)
    for d in range(1, NGY):
        pl.semaphore_signal(barrier, inc=1, device_id=(lax.rem(j + d, NGY), i), device_id_type=MESH)

    n = lanes((128, 512))
    c = lax.broadcasted_iota(jnp.int32, (128, 512), 0)
    matrix = jnp.where(c == 4 * (n & 127) + (n >> 7), 1.0, 0.0).astype(jnp.bfloat16)
    blocks = jnp.concatenate([phase[0], phase[1], velocity[0], velocity[1]], axis=0)
    split = permuted(blocks, matrix)
    for k in range(4):
        u, v = (split[64 * f : 64 * f + 64, 128 * k : 128 * k + 128] for f in range(2))
        u, v = (cut[:32] + lane_roll(cut[32:], 64) for cut in (u, v))
        u = u + lane_roll(v, 32)
        for g in range(4):
            own[pl.ds(64 * (g // 2) + 4 * (g % 2) + k, 8, stride=8), :] = u[8 * g : 8 * g + 8]

    pl.semaphore_wait(barrier, NGX - 1 + NGY - 1)
    to_row(own, got, ssem.at[0], rsem.at[0])
    for row in (up, down, up2, down2):
        pl.semaphore_signal(ready, inc=1, device_id=(row, i), device_id_type=MESH)
    pending.append(all_tiles(got, 31, ssem.at[0], rsem.at[0]).wait_send)
    to_sides(own, west, east, 1)
    pending.append(all_tiles(own, 16, ssem.at[1], rsem.at[1]).wait_send)
    pending.append(all_tiles(own, 16, ssem.at[2], rsem.at[2]).wait_send)
    for ref in (window, ahead, window2):
        for p in range(8):
            for at in (16 * p, 16 * (56 + p) + 8):
                ref[at : at + 8, :] = jnp.zeros((8, 128), jnp.float32)
    all_tiles(got, 31, ssem.at[0], rsem.at[0]).wait_recv()
    to_spread(got)
    pl.semaphore_wait(ready, 4)
    to_columns(sent, window, 0, ssem.at[3], rsem.at[3])
    pending.append(lambda: columns_sent(sent, ssem.at[3], rsem.at[3]))
    to_columns(later, ahead, 1, ssem.at[4], rsem.at[4])
    pending.append(lambda: columns_sent(later, ssem.at[4], rsem.at[4]))
    all_tiles(west, 16, ssem.at[1], rsem.at[1]).wait_recv()
    all_tiles(east, 16, ssem.at[2], rsem.at[2]).wait_recv()
    own_windows(own, west, east, (window, ahead))
    all_tiles(window, 80, ssem.at[3], rsem.at[3]).wait_recv()

    def solve(u, v):
        r = residual_of(u, v)
        w = precondition(r)
        q = operate(w)
        z = precondition(q)
        return r, w, q, z

    def sums_of(r, w, q, z):
        return packed_sums(((r, w), (w, q), (r, z), (q, z), (z, operate(z))))

    r, w, q, z = solve(rows_of(window, 0), rows_of(window, 1))
    put_rows(stage, 0, w)
    put_rows(stage, 1, z)
    m = lanes() & 63
    for p in range(16):
        at = 16 * (24 + p)
        first, second = by_row(stage[at : at + 8, :], stage[at + 8 : at + 16, :])
        own2[8 * p : 8 * p + 8, :] = jnp.where(m < 32, lane_roll(first, 112), lane_roll(second, 16))
    to_row(own2, got2, ssem.at[5], rsem.at[5])
    pending.append(all_tiles(got2, 31, ssem.at[5], rsem.at[5]).wait_send)
    sums_to_row(sums_of(r, w, q, z), part, sums_row, 0)
    pending.append(few(sums_row, 31, 0).wait_send)
    to_sides(own2, west2, east2, 6)
    pending.append(all_tiles(own2, 16, ssem.at[6], rsem.at[6]).wait_send)
    pending.append(all_tiles(own2, 16, ssem.at[7], rsem.at[7]).wait_send)
    all_tiles(got2, 31, ssem.at[5], rsem.at[5]).wait_recv()
    to_spread(got2)
    to_columns(third, window2, 1, ssem.at[8], rsem.at[8])
    pending.append(lambda: columns_sent(third, ssem.at[8], rsem.at[8]))
    few(sums_row, 31, 0).wait_recv()
    sums_to_col(jnp.sum(sums_row[...], axis=0), part_row, sums_col, 1)
    pending.append(few(sums_col, 7, 1).wait_send)
    all_tiles(west2, 16, ssem.at[6], rsem.at[6]).wait_recv()
    all_tiles(east2, 16, ssem.at[7], rsem.at[7]).wait_recv()
    own_windows(own2, west2, east2, (window2,))
    few(sums_col, 7, 1).wait_recv()
    c1, c2 = coefficients(jnp.sum(sums_col[...], axis=0))
    all_tiles(ahead, 80, ssem.at[4], rsem.at[4]).wait_recv()
    all_tiles(window2, 80, ssem.at[8], rsem.at[8]).wait_recv()

    def moved(u, w, z, c1, c2):
        return [a + 0.5 * mixed(c1 * b + c2 * d) for a, b, d in zip(u, w, z)]

    u = moved(rows_of(ahead, 0), rows_of(window2, 0), rows_of(window2, 1), c1, c2)
    r, w, q, z = solve(u, rows_of(ahead, 1))
    packed = sums_of(r, w, q, z)
    part2[...] = packed
    to_core = copy(part2, sums2_core, s2sem.at[2], r2sem.at[2], j + 1 - 2 * lax.rem(j, 2), i)
    to_core.start()
    pending.append(to_core.wait_send)
    put_rows(stage, 0, u)
    put_rows(window, 0, w)
    put_rows(window, 1, z)
    to_core.wait_recv()
    total = packed + sums2_core[...]
    part2_chip[...] = total
    chip_y = j // 2
    sums2[chip_y * NGX + i] = total

    def to_chips(n, carry):
        y, c = lax.rem(chip_y + n // NGX, 4), lax.rem(i + n, NGX)
        copy(part2_chip, sums2.at[chip_y * NGX + i], s2sem.at[3], r2sem.at[3], 2 * y + lax.rem(j, 2), c).start()
        return carry

    lax.fori_loop(1, 128, to_chips, 0)
    pending.append(few(sums2, 127, 3).wait_send)
    flat = jnp.concatenate(
        [
            jnp.concatenate(
                [
                    ref[pl.ds(16 * (24 + 8 * (g // 2)) + 8 * (g % 2) + 4 * f + k, 8, stride=16), :]
                    for ref, f in ((stage, 0), (window, 0), (window, 1))
                    for g in range(4)
                ],
                axis=0,
            )
            for k in range(4)
        ],
        axis=1,
    )
    rho = lax.broadcasted_iota(jnp.int32, (512, 256), 0)
    col = lanes((512, 256))
    c = col & 127
    same = ((rho >> 7) == (c & 3)) & ((rho & 63) == 16 + (c >> 2))
    plane, of_plane = (rho >> 6) & 1, col >> 7
    straight = jnp.where(same & (plane == of_plane), 1.0, 0.0).astype(jnp.bfloat16)
    halves = jnp.where(same, jnp.where(plane + of_plane == 2, -0.5, 0.5), 0.0).astype(jnp.bfloat16)
    u = permuted(flat[:32], straight)
    wz = permuted(flat[32:], halves)
    few(sums2, 127, 3).wait_recv()
    c1, c2 = coefficients(jnp.sum(sums2[...], axis=0))
    flat = u + c1 * wz[:32] + c2 * wz[32:]
    out[0] = flat[:, :128]
    out[1] = flat[:, 128:]

    for wait in pending:
        wait()


def local(phase, velocity, offsets):
    f32 = jnp.float32
    tiles = lambda count: pltpu.VMEM((8 * count, 128), f32)
    line, lines = pltpu.VMEM((1, 128), f32), lambda n: pltpu.VMEM((n, 1, 128), f32)
    vmem = pl.BlockSpec(memory_space=pltpu.VMEM)
    return pl.pallas_call(
        kernel,
        out_shape=jax.ShapeDtypeStruct(phase.shape, f32),
        in_specs=[pl.BlockSpec(memory_space=pltpu.SMEM), vmem, vmem],
        out_specs=vmem,
        scratch_shapes=[
            tiles(16), tiles(32), tiles(64), tiles(16), tiles(16), tiles(192), tiles(192), tiles(192), tiles(128), tiles(128), tiles(128),
            tiles(16), tiles(32), tiles(16), tiles(16), tiles(128),
            line, line, lines(32), lines(8), line, line, line, lines(128),
            pltpu.SemaphoreType.DMA((9,)), pltpu.SemaphoreType.DMA((9,)),
            pltpu.SemaphoreType.DMA((4,)), pltpu.SemaphoreType.DMA((4,)), pltpu.SemaphoreType.REGULAR,
        ],
        compiler_params=pltpu.CompilerParams(collective_id=0, has_side_effects=True),
    )(offsets, phase, velocity)


def solution(mesh):
    return jax.shard_map(
        local,
        mesh=mesh,
        in_specs=(P(None, "gy", "gx"), P(None, "gy", "gx"), P()),
        out_specs=P(None, "gy", "gx"),
        check_vma=False,
    )
```
